128 devices in a mesh: fft: 32 (over z, x, core), chan: 4 (over y).
Axes of the slice: x: 4, y: 4, z: 4, core: 2. Of those that a mesh axis runs over, the one named last changes fastest.
Arguments:
- visibilities: float32 [128, 2, 128, 128], P(('fft', 'chan')), may hold values from -6 to 6
- positions: float32 [128, 2, 128, 128], P(('fft', 'chan')), may hold values from 0 to 1
- cell_row: int32 [128, 128, 128], P(('fft', 'chan')), may hold values from 4 to 59
- cell_column: int32 [128, 128, 128], P(('fft', 'chan')), may hold values from 4 to 251
- kernel_class: int32 [128, 128, 128], P(('fft', 'chan')), may hold values from 0 to 3
- send_counts: int32 [128, 128], P(('fft', 'chan')), may hold values from 96 to 128, as said below
- tile_lists: int32 [128, 8, 1536], P(('fft', 'chan')), may hold values from 0 to 16383, as said below
- tile_counts: int32 [128, 8], P(('fft', 'chan')), may hold values from 768 to 1536, as said below
- model_image: float32 [8, 128, 32768], P('chan', 'fft'), may hold values from -6 to 6
- threshold: float32 [8], P('chan'), may hold values from 0.5 to 3
Outputs:
- updated_model: float32 [8, 128, 32768], P('chan', 'fft')
- residuals: float32 [128, 2, 128, 128], P(('fft', 'chan'))
The draws below stay inside these ranges and needn't reach their ends.
Inputs may be any that keep to these rules, and one draw needn't show every extreme that they name: `send_counts`: for each receiver some sender uses all 128 slots to it. `tile_lists`: entries below a list's count name slots p of sender s with p < send_counts[s, d] for the receiver d, and no slot is named twice among the entries below the counts of one receiver; other entries are arbitrary slot numbers. `tile_counts`: on every receiver one list has exactly 1536 entries in use.
All inputs are finite; a program needn't handle non-finite values.
Results may differ from the reference program's by a relative error of at most 0.0003.
Values sent between devices are 32-bit elements; how exact they have to be, the bound alone decides.
No kernel may reach another device: no remote copies, remote signals or barrier semaphores. Data moves between devices by JAX's collectives and lax.ppermute only.
A program may use at most 192 MiB of HBM per device.

```python
import math
import jax
import jax.numpy as jnp
from jax import lax

V_LEN = 32768
BU = 64
FACET = 128
CH_DEV = 2
CH = 8
TPD = 4
TV = 256
TILES = 128
TLOC = 8
NW = 4
PER = 128
SENDERS = 128
TILE_CAP = 1536
N_FFT = 32
N_CHAN = 4


def routing_tables(key):
    base_key = jax.random.fold_in(key, 4242)
    key_list = jax.random.split(base_key, 5)
    slot_total = SENDERS * PER
    counts = jax.random.randint(key_list[0], (SENDERS, SENDERS), 3 * PER // 4, PER + 1)
    full_source = jax.random.randint(key_list[1], (SENDERS,), 0, SENDERS)
    counts = jnp.where(jnp.arange(SENDERS, dtype=jnp.int32)[:, None] == full_source[None, :], PER, counts)
    slot_ids = jnp.arange(slot_total, dtype=jnp.int32)
    usable = slot_ids[None, :] % PER < jnp.repeat(counts.T, PER, axis=1)
    ranks = jax.vmap(lambda one_key: jax.random.permutation(one_key, slot_total))(jax.random.split(key_list[2], SENDERS))
    ranks = ranks.astype(jnp.int32)
    scores = jnp.where(usable, ranks, ranks + slot_total)
    ordering = jnp.argsort(scores, axis=1, stable=True).astype(jnp.int32)
    loads = jax.random.randint(key_list[3], (SENDERS, TLOC), TILE_CAP // 2, TILE_CAP + 1)
    heavy = jax.random.randint(key_list[4], (SENDERS,), 0, TLOC)
    loads = jnp.where(jnp.arange(TLOC, dtype=jnp.int32)[None, :] == heavy[:, None], TILE_CAP, loads)
    starts = jnp.cumsum(loads, axis=1) - loads
    picks = (starts[:, :, None] + jnp.arange(TILE_CAP, dtype=jnp.int32)[None, None, :]) % slot_total
    lists = jnp.take_along_axis(ordering, picks.reshape(SENDERS, TLOC * TILE_CAP), axis=1)
    lists = lists.reshape(SENDERS, TLOC, TILE_CAP).astype(jnp.int32)
    return (counts.astype(jnp.int32), lists, loads.astype(jnp.int32))


def draw_send_counts(key, part):
    return routing_tables(key)[0]


def draw_tile_lists(key, part):
    return routing_tables(key)[1]


def draw_tile_counts(key, part):
    return routing_tables(key)[2]


def set_ends(entries, stream_key, low, high):
    longest = entries.shape.index(max(entries.shape))
    spots = []
    for shift in (0, 1):
        where = [jax.random.randint(jax.random.fold_in(stream_key, axis), (), 0, length) for axis, length in enumerate(entries.shape)]
        where[longest] = (where[longest] + shift) % entries.shape[longest]
        spots.append(tuple(where))
    return entries.at[spots[0]].set(low).at[spots[1]].set(high)


def block_levels(key, dims, cuts, low, top_value):
    level = 1.0
    for axis_at, shards_of in cuts:
        heights = jax.random.uniform(jax.random.fold_in(jax.random.fold_in(key, 6), axis_at), (shards_of,), jnp.float32, low / len(cuts), top_value / len(cuts))
        level = level * jnp.repeat(jnp.exp(heights), dims[axis_at] // shards_of).reshape((-1,) + (1,) * (len(dims) - 1 - axis_at))
    return level


def centred(rng, dims, scale, reach, cuts=(), held_as=jnp.bfloat16):
    drawn = jax.random.normal(rng, dims, jnp.float32) * scale
    if len(cuts) > 0:
        drawn = block_levels(rng, dims, cuts, -0.22, 0.18) * drawn
    return jnp.clip(drawn, min=-reach, max=reach).astype(held_as)


def setup_inputs(seed: int = 0) -> dict:
    key_of = jax.random.split(jax.random.key(seed), 11)
    return {
        "visibilities": centred(key_of[0], (SENDERS, 2, SENDERS, PER), 1.0, 6.0, ((0, 128),), jnp.float32),
        "positions": jnp.clip(1.0 * jax.random.uniform(key_of[1], (SENDERS, 2, SENDERS, PER), jnp.float32) ** block_levels(key_of[1], (SENDERS, 2, SENDERS, PER), ((0, 128),), -0.2, 0.2), 0.0, 1.0),
        "cell_row": set_ends(jax.random.randint(key_of[2], (SENDERS, SENDERS, PER), NW, BU - NW), jax.random.fold_in(key_of[2], 1), NW, (BU - NW) - 1).astype(jnp.int32),
        "cell_column": set_ends(jax.random.randint(key_of[3], (SENDERS, SENDERS, PER), NW, TV - NW), jax.random.fold_in(key_of[3], 1), NW, (TV - NW) - 1).astype(jnp.int32),
        "kernel_class": set_ends(jax.random.randint(key_of[4], (SENDERS, SENDERS, PER), 0, NW), jax.random.fold_in(key_of[4], 1), 0, NW - 1).astype(jnp.int32),
        "send_counts": draw_send_counts(jax.random.fold_in(key_of[10], 71), 0),
        "tile_lists": draw_tile_lists(jax.random.fold_in(key_of[10], 71), 0),
        "tile_counts": draw_tile_counts(jax.random.fold_in(key_of[10], 71), 0),
        "model_image": centred(key_of[8], (CH, FACET, V_LEN), 1.0, 6.0, ((0, 4), (1, 32)), jnp.float32),
        "threshold": jnp.clip(jnp.exp(math.log(3.0) - 1.7917595 * jax.random.uniform(key_of[9], (CH,), jnp.float32) ** block_levels(key_of[9], (CH,), ((0, 4),), -0.2, 0.2)), 0.5, 3.0),
    }


LOOP_GAIN = 0.7
EXACT_ARITHMETIC = lax.Precision.HIGHEST

def kernel_table(center_cell, fraction, class_index, length):
    grid_cells = jnp.arange(length, dtype=jnp.int32)
    distance = grid_cells[None, :] - center_cell[:, None]
    half_width = class_index + 1
    inside = jnp.abs(distance) <= half_width[:, None]
    spread = 0.6 * half_width.astype(jnp.float32)
    offset = distance.astype(jnp.float32) - fraction[:, None]
    shape_value = jnp.exp(-offset * offset / (2.0 * spread[:, None] * spread[:, None]))
    return jnp.where(inside, shape_value, jnp.zeros_like(shape_value))

def band_phases(band_rows, image_rows, grid_side):
    row_index = jnp.arange(band_rows, dtype=jnp.int32)
    image_index = jnp.arange(image_rows, dtype=jnp.int32)
    phase_index = (grid_side // 2 + row_index)[None, :] * image_index[:, None] % image_rows
    angle = -2.0 * math.pi / image_rows * phase_index.astype(jnp.float32)
    return (jnp.cos(angle), jnp.sin(angle))

def listed_entries(dest, visibilities, positions, cell_row, cell_column, kernel_class, tile_lists, tile_counts):
    slot_lists = tile_lists[dest]
    source = slot_lists // PER
    slot_index = slot_lists % PER
    listed = (jnp.arange(TILE_CAP, dtype=jnp.int32)[None, :] < tile_counts[dest][:, None]).astype(jnp.float32)
    values = visibilities[source, :, dest, slot_index]
    fraction = positions[source, :, dest, slot_index]
    classes = kernel_class[source, dest, slot_index].reshape(-1)
    row_kernel = kernel_table(cell_row[source, dest, slot_index].reshape(-1), fraction[..., 0].reshape(-1), classes, BU)
    column_kernel = kernel_table(cell_column[source, dest, slot_index].reshape(-1), fraction[..., 1].reshape(-1), classes, TV)
    row_kernel = row_kernel.reshape(TLOC, TILE_CAP, BU)
    column_kernel = column_kernel.reshape(TLOC, TILE_CAP, TV)
    return (source, slot_index, listed, values, row_kernel, column_kernel)

def reference(visibilities, positions, cell_row, cell_column, kernel_class, send_counts, tile_lists, tile_counts, model_image, threshold):
    dirty_scale = 1.0 / math.sqrt(TILES * TILE_CAP)
    back_scale = 0.5 / math.sqrt(FACET * V_LEN)

    def grid_device(dest):
        source, slot_index, listed, values, row_kernel, column_kernel = listed_entries(dest, visibilities, positions, cell_row, cell_column, kernel_class, tile_lists, tile_counts)
        weights = jnp.moveaxis(values, 2, 0) * listed[None]
        weighted = row_kernel[None] * weights[..., None]
        return jnp.einsum('ctku,tkv->ctuv', weighted, column_kernel, precision=EXACT_ARITHMETIC)
    tiles = lax.map(grid_device, jnp.arange(SENDERS, dtype=jnp.int32))
    channel_grid = tiles.reshape(N_FFT, N_CHAN, 2, CH_DEV, TPD, BU, TV).transpose(2, 1, 3, 5, 0, 4, 6)
    channel_grid = channel_grid.reshape(2, CH, BU, V_LEN)
    band_cos, band_sin = band_phases(BU, FACET, V_LEN)

    def image_channel(item):
        grid_re, grid_im, prior, clip_level = item
        spectrum = jnp.fft.fft(grid_re + 1j * grid_im, axis=1)
        spec_re = jnp.real(spectrum)
        spec_im = jnp.imag(spectrum)
        dirty_image = (jnp.dot(band_cos, spec_re, precision=EXACT_ARITHMETIC) - jnp.dot(band_sin, spec_im, precision=EXACT_ARITHMETIC)) * dirty_scale
        updated = prior + LOOP_GAIN * (dirty_image - jnp.clip(dirty_image, -clip_level, clip_level))
        inverse = jnp.fft.ifft(updated, axis=1) * V_LEN
        inv_re = jnp.real(inverse)
        inv_im = jnp.imag(inverse)
        pred_re = (jnp.dot(band_cos.T, inv_re, precision=EXACT_ARITHMETIC) + jnp.dot(band_sin.T, inv_im, precision=EXACT_ARITHMETIC)) * back_scale
        pred_im = (jnp.dot(band_cos.T, inv_im, precision=EXACT_ARITHMETIC) - jnp.dot(band_sin.T, inv_re, precision=EXACT_ARITHMETIC)) * back_scale
        return (updated, jnp.stack([pred_re, pred_im]))
    updated_model, predicted = lax.map(image_channel, (channel_grid[0], channel_grid[1], model_image, threshold))
    predicted = predicted.transpose(1, 0, 2, 3).reshape(2, N_CHAN, CH_DEV, BU, N_FFT, TPD, TV)
    tile_grids = predicted.transpose(4, 1, 0, 2, 5, 3, 6).reshape(SENDERS, 2, TLOC, BU, TV)

    def degrid_device(item):
        dest, grids = item
        source, slot_index, listed, values, row_kernel, column_kernel = listed_entries(dest, visibilities, positions, cell_row, cell_column, kernel_class, tile_lists, tile_counts)
        partial_value = jnp.einsum('tku,ctuv->ctkv', row_kernel, grids, precision=EXACT_ARITHMETIC)
        predicted_slot = lax.optimization_barrier(jnp.sum(partial_value * column_kernel[None], axis=3)) * listed[None]
        received = jnp.zeros((2, SENDERS, PER), jnp.float32)
        return received.at[:, source, slot_index].add(predicted_slot)
    returned = lax.map(degrid_device, (jnp.arange(SENDERS, dtype=jnp.int32), tile_grids))
    returned = returned.transpose(2, 1, 0, 3)
    sent_live = jnp.arange(PER, dtype=jnp.int32)[None, None, :] < send_counts[:, :, None]
    residuals = jnp.where(sent_live[:, None], visibilities - returned, jnp.zeros_like(visibilities))
    return (updated_model, residuals)
```

```python
import math

import jax
import jax.numpy as jnp
import numpy as np
from jax import lax
from jax.experimental import pallas as pl
from jax.experimental.pallas import tpu as pltpu
from jax.sharding import PartitionSpec as P

BU = 64
LOOP_GAIN = 0.7
N1 = 128
N2 = 256
CHUNK = 256
LANES = 128
F32 = jnp.float32
BF16 = jnp.bfloat16
GAUSS = math.sqrt(1.0 / (0.72 * math.log(2.0)))
VMEM_BYTES = 60 * 1024 * 1024

NN = (((1,), (0,)), ((), ()))
NT = (((1,), (1,)), ((), ()))
TN = (((0,), (0,)), ((), ()))


def split(x):
    high = x.astype(BF16)
    low = (x - high.astype(F32)).astype(BF16)
    return high, low


def mm(a, b, dims):
    return lax.dot_general(a, b, dims, preferred_element_type=F32)


def mm3(a, b, dims):
    return mm(a[0], b[0], dims) + (mm(a[1], b[0], dims) + mm(a[0], b[1], dims))


def np_split(x):
    x = np.asarray(x, np.float32)
    high = x.astype(jnp.bfloat16)
    low = (x - high.astype(np.float32)).astype(jnp.bfloat16)
    return np.stack([high, low])


def angles(rows, cols, modulus):
    product = np.arange(rows, dtype=np.int64)[:, None] * np.arange(cols, dtype=np.int64)[None, :] % modulus
    return 2.0 * np.pi / modulus * product


def tables(facet_rows, row_local, grid_side, dirty_scale, back_scale):
    phase = (grid_side // 2 + np.arange(BU))[None, :] * np.arange(facet_rows)[:, None] % facet_rows
    theta = 2.0 * np.pi / facet_rows * phase
    c, s = np.cos(theta), np.sin(theta)
    owners = facet_rows // row_local
    forward = np.zeros((owners, 2, row_local, 2, BU))
    cc, ss = c.reshape(owners, row_local, BU), s.reshape(owners, row_local, BU)
    forward[:, 0, :, 0], forward[:, 0, :, 1] = cc, ss
    forward[:, 1, :, 0], forward[:, 1, :, 1] = -ss, cc
    forward = forward.reshape(2 * facet_rows, 2 * BU)
    backward = forward.T * back_scale
    forward = forward * dirty_scale
    a = angles(N1, N1, N1)
    c, s = np.cos(a), np.sin(a)
    lead = np.block([[c, -s], [s, c]])
    a = angles(N2, N2, N2)
    tail = np.concatenate([np.cos(a), np.sin(a)], axis=1)
    tail_back = np.concatenate([np.cos(a), np.sin(a)], axis=0)
    a = angles(N2, N1, N1 * N2)
    twist = np.stack([np.cos(a), np.sin(a)]).astype(np.float32)
    return {
        "forward": np_split(forward),
        "backward": np_split(backward),
        "lead": np_split(lead),
        "tail": np_split(tail),
        "tail_back": np_split(tail_back),
        "twist": twist,
    }


def gauss(cell, centre, half, scale, length):
    line = lax.broadcasted_iota(jnp.int32, (length, cell.shape[1]), 0).astype(F32)
    y = (line - centre) * scale
    return jnp.where(jnp.abs(line - cell) <= half, jnp.exp2(-(y * y)), 0.0)


def pack_body(vis, pos, row, col, cls, out):
    rows = row.shape[0]
    for part in range(2):
        out[pl.ds(part, rows, stride=8), :] = vis[part]
        out[pl.ds(2 + part, rows, stride=8), :] = pos[part]
    out[pl.ds(4, rows, stride=8), :] = row[...].astype(F32)
    out[pl.ds(5, rows, stride=8), :] = col[...].astype(F32)
    out[pl.ds(6, rows, stride=8), :] = cls[...].astype(F32)
    out[pl.ds(7, rows, stride=8), :] = jnp.zeros((rows, row.shape[1]), F32)


def pack(vis, pos, row, col, cls):
    return pl.pallas_call(
        pack_body,
        out_shape=jax.ShapeDtypeStruct((8 * row.shape[0], row.shape[1]), F32),
        name="pack",
    )(vis, pos, row, col, cls)


def grid_kernel_body(counts, lists, got, forward, out, feats, tab, *, base):
    r = pl.program_id(0)
    senders = got.shape[0] // 8
    slots = got.shape[1]

    @pl.when(r == 0)
    def _():
        for k in range(4):
            high, low = split(got[pl.ds(k, senders, stride=8), :])
            tab[k * senders : (k + 1) * senders, 0:slots] = high
            tab[k * senders : (k + 1) * senders, slots : 2 * slots] = low
        row = got[pl.ds(4, senders, stride=8), :]
        col = got[pl.ds(5, senders, stride=8), :]
        cls = got[pl.ds(6, senders, stride=8), :]
        tab[4 * senders : 5 * senders, 0:slots] = ((row * 4.0 + cls) * 256.0).astype(BF16)
        tab[4 * senders : 5 * senders, slots : 2 * slots] = col.astype(BF16)

    count = counts[base + r]
    chunks = lists.shape[1] // CHUNK
    live_chunks = (count + (CHUNK - 1)) // CHUNK
    line = lax.broadcasted_iota(jnp.int32, (senders, CHUNK), 0)
    tick = lax.broadcasted_iota(jnp.int32, (1, CHUNK), 1)

    def step(j, acc):
        start = pl.multiple_of(j * CHUNK, CHUNK)
        slot = lists[:, pl.ds(start, CHUNK)]
        sender = lax.shift_right_logical(slot, 7)
        place = lax.bitwise_and(slot, slots - 1)
        pick = jnp.where(line == place, 1.0, 0.0).astype(BF16)
        picks = jnp.concatenate([pick, pick], axis=0)
        found = mm(tab[...], picks, NN)
        mine = line == sender
        vals = [
            jnp.sum(jnp.where(mine, found[k * senders : (k + 1) * senders], 0.0), axis=0, keepdims=True)
            for k in range(5)
        ]
        live = (start + tick) < count
        code = vals[4].astype(jnp.int32)
        cell_col = lax.bitwise_and(code, 255).astype(F32)
        cell_row = lax.shift_right_logical(code, 10).astype(F32)
        half = lax.bitwise_and(lax.shift_right_logical(code, 8), 3).astype(F32) + 1.0
        scale = GAUSS / half
        vr = jnp.where(live, vals[0], 0.0)
        vi = jnp.where(live, vals[1], 0.0)
        row_centre = cell_row + vals[2]
        col_centre = cell_col + vals[3]
        zero = jnp.zeros_like(scale)
        feats[:, pl.ds(start, CHUNK)] = jnp.concatenate(
            [cell_row, row_centre, cell_col, col_centre, half, scale, zero, zero], axis=0
        )
        rows = gauss(cell_row, row_centre, half, scale, BU)
        cols = split(gauss(cell_col, col_centre, half, scale, N2))
        weighted = split(jnp.concatenate([rows * vr, rows * vi], axis=0))
        return acc + mm3(weighted, cols, NT)

    acc = lax.fori_loop(0, live_chunks, step, jnp.zeros((2 * BU, N2), F32))
    bands = mm3((forward[0], forward[1]), split(acc), NN)
    for h in range(2):
        out[:, h] = bands[:, h * LANES : (h + 1) * LANES].reshape(out.shape[0], 8, LANES)


def grid_channel(counts, lists, got, forward, channel, tiles, owners):
    local, cap = lists.shape
    base = channel * tiles
    spec = pltpu.PrefetchScalarGridSpec(
        num_scalar_prefetch=1,
        grid=(tiles,),
        in_specs=[
            pl.BlockSpec((None, 1, cap), lambda r, c: (base + r, 0, 0)),
            pl.BlockSpec(got.shape, lambda r, c: (0, 0)),
            pl.BlockSpec(forward.shape, lambda r, c: (0, 0, 0)),
        ],
        out_specs=[
            pl.BlockSpec((owners, None, 2, 8, LANES), lambda r, c: (0, r, 0, 0, 0)),
            pl.BlockSpec((None, 8, cap), lambda r, c: (r, 0, 0)),
        ],
        scratch_shapes=[pltpu.VMEM((5 * got.shape[0] // 8, 2 * got.shape[1]), BF16)],
    )

    def body(*refs):
        grid_kernel_body(*refs, base=base)

    return pl.pallas_call(
        body,
        grid_spec=spec,
        out_shape=[
            jax.ShapeDtypeStruct((owners, tiles, 2, 8, LANES), F32),
            jax.ShapeDtypeStruct((tiles, 8, cap), F32),
        ],
        compiler_params=pltpu.CompilerParams(vmem_limit_bytes=VMEM_BYTES),
        name="grid_tiles",
    )(counts, lists.reshape(local, 1, cap), got, forward)


def transform_body(clip, got, model, lead, tail, tail_back, twist, updated, out, *, channel, rows):
    level = clip[channel]
    tc, ts = twist[0], twist[1]
    lead_parts = (lead[0], lead[1])
    for l in range(rows):
        parts = [
            jnp.concatenate([got[pl.ds(h * 8 + part * rows + l, N1, stride=16), :] for h in range(2)], axis=1)
            for part in range(2)
        ]
        x = jnp.concatenate(parts, axis=0)
        y = mm3(split(x), lead_parts, TN)
        yr, yi = y[:, :N1], y[:, N1:]
        turned = jnp.concatenate([yr * tc + yi * ts, yi * tc - yr * ts], axis=0)
        dirty = mm3((tail[0], tail[1]), split(turned), NN)
        prior = model[pl.ds(l, N2, stride=rows), :]
        new = prior + LOOP_GAIN * (dirty - jnp.clip(dirty, -level, level))
        updated[pl.ds(l, N2, stride=rows), :] = new
        a = mm3((tail_back[0], tail_back[1]), split(new), NN)
        ar, ai = a[:N2], a[N2:]
        turned = jnp.concatenate([ar * tc - ai * ts, ar * ts + ai * tc], axis=1)
        z = mm3(lead_parts, split(turned), NT)
        for part in range(2):
            for h in range(2):
                out[pl.ds(h * 8 + part * rows + l, N1, stride=16), :] = z[
                    part * N1 : (part + 1) * N1, h * LANES : (h + 1) * LANES
                ]


def transform_channel(clip, got, model, consts, channel, rows):
    def body(*refs):
        transform_body(*refs, channel=channel, rows=rows)

    whole = pl.BlockSpec(memory_space=pltpu.VMEM)
    return pl.pallas_call(
        body,
        in_specs=[pl.BlockSpec(memory_space=pltpu.SMEM)] + [whole] * 6,
        out_specs=[whole, whole],
        out_shape=[
            jax.ShapeDtypeStruct(model.shape, F32),
            jax.ShapeDtypeStruct(got.shape, F32),
        ],
        compiler_params=pltpu.CompilerParams(vmem_limit_bytes=VMEM_BYTES),
        name="transform",
    )(clip, got, model, consts["lead"], consts["tail"], consts["tail_back"], consts["twist"])


def degrid_body(counts, lists, feats, got, backward, prior, out, acc_ref, *, base):
    r = pl.program_id(0)
    senders = prior.shape[0] // 2
    slots = prior.shape[1]

    @pl.when(r == 0)
    def _():
        acc_ref[...] = jnp.zeros_like(acc_ref)

    count = counts[base + r]
    live_chunks = (count + (CHUNK - 1)) // CHUNK
    line = lax.broadcasted_iota(jnp.int32, (senders, CHUNK), 0)
    tick = lax.broadcasted_iota(jnp.int32, (1, CHUNK), 1)
    columns = jnp.concatenate([got[:, h].reshape(got.shape[0] * 8, LANES) for h in range(2)], axis=1)
    pred = mm3((backward[0], backward[1]), split(columns), NN)
    ph, pw = split(pred)

    def step(j, acc):
        start = pl.multiple_of(j * CHUNK, CHUNK)
        slot = lists[:, pl.ds(start, CHUNK)]
        sender = lax.shift_right_logical(slot, 7)
        place = lax.bitwise_and(slot, slots - 1)
        live = (start + tick) < count
        feat = feats[:, pl.ds(start, CHUNK)]
        rows = gauss(feat[0:1], feat[1:2], feat[4:5], feat[5:6], BU)
        ch, cl = split(gauss(feat[2:3], feat[3:4], feat[4:5], feat[5:6], N2))
        t = mm(ph, ch, NN) + (mm(pw, ch, NN) + mm(ph, cl, NN))
        pick = jnp.where(line == place, 1.0, 0.0).astype(BF16)
        mine = line == sender
        sides = []
        for part in range(2):
            val = jnp.sum(t[part * BU : (part + 1) * BU] * rows, axis=0, keepdims=True)
            val = jnp.where(live, val, 0.0)
            high = val.astype(BF16).astype(F32)
            low = val - high
            sides.append(jnp.where(mine, high, 0.0).astype(BF16))
            sides.append(jnp.where(mine, low, 0.0).astype(BF16))
        spread = mm(jnp.concatenate(sides, axis=0), pick, NT)
        return acc + spread

    acc_ref[...] = lax.fori_loop(0, live_chunks, step, acc_ref[...])

    @pl.when(r == pl.num_programs(0) - 1)
    def _():
        for part in range(2):
            lo = 2 * part * senders
            total = acc_ref[lo : lo + senders] + acc_ref[lo + senders : lo + 2 * senders]
            out[pl.ds(part, senders, stride=2), :] = prior[pl.ds(part, senders, stride=2), :] + total


def degrid_channel(counts, lists, feats, got, backward, prior, channel):
    owners, tiles = got.shape[:2]
    local, cap = lists.shape
    base = channel * tiles
    spec = pltpu.PrefetchScalarGridSpec(
        num_scalar_prefetch=1,
        grid=(tiles,),
        in_specs=[
            pl.BlockSpec((None, 1, cap), lambda r, c: (base + r, 0, 0)),
            pl.BlockSpec((None, 8, cap), lambda r, c: (r, 0, 0)),
            pl.BlockSpec((owners, None, 2, 8, LANES), lambda r, c: (0, r, 0, 0, 0)),
            pl.BlockSpec(backward.shape, lambda r, c: (0, 0, 0)),
            pl.BlockSpec(prior.shape, lambda r, c: (0, 0)),
        ],
        out_specs=pl.BlockSpec(prior.shape, lambda r, c: (0, 0)),
        scratch_shapes=[pltpu.VMEM((2 * prior.shape[0], prior.shape[1]), F32)],
    )

    def body(*refs):
        degrid_body(*refs, base=base)

    return pl.pallas_call(
        body,
        grid_spec=spec,
        out_shape=jax.ShapeDtypeStruct(prior.shape, F32),
        compiler_params=pltpu.CompilerParams(vmem_limit_bytes=VMEM_BYTES),
        name="degrid_tiles",
    )(counts, lists.reshape(local, 1, cap), feats, got, backward, prior)


def finish_body(vis, got, counts, out):
    rows, slots = got.shape[0] // 2, got.shape[1]
    limit = jnp.broadcast_to(counts[...], (rows, rows)).T[:, :slots]
    lane = lax.broadcasted_iota(jnp.int32, (rows, slots), 1)
    for part in range(2):
        diff = vis[part] - got[pl.ds(part, rows, stride=2), :]
        out[part] = jnp.where(lane < limit, diff, 0.0)


def finish(vis, got, counts):
    return pl.pallas_call(
        finish_body,
        out_shape=jax.ShapeDtypeStruct(vis.shape, F32),
        name="finish",
    )(vis, got, counts)


def per_device(
    visibilities,
    positions,
    cell_row,
    cell_column,
    kernel_class,
    send_counts,
    tile_lists,
    tile_counts,
    model_image,
    threshold,
):
    owners = lax.axis_size("fft")
    senders = owners * lax.axis_size("chan")
    slots = visibilities.shape[3]
    channels, row_local, grid_side = model_image.shape
    cap = tile_lists.shape[2]
    tiles = tile_lists.shape[1] // channels
    facet_rows = row_local * owners
    dirty_scale = 1.0 / math.sqrt(owners * tiles * cap)
    back_scale = 0.5 / math.sqrt(facet_rows * grid_side)
    consts = {k: jnp.asarray(v) for k, v in tables(facet_rows, row_local, grid_side, dirty_scale, back_scale).items()}
    lists, counts = tile_lists[0], tile_counts[0]

    payload = pack(visibilities[0], positions[0], cell_row[0], cell_column[0], kernel_class[0])
    got = lax.all_to_all(
        payload.reshape(senders, 8, slots), ("fft", "chan"), split_axis=0, concat_axis=0, tiled=True
    ).reshape(8 * senders, slots)

    def exchange(x):
        return lax.all_to_all(x, "fft", split_axis=0, concat_axis=0, tiled=True)

    models = model_image.reshape(channels, row_local, N2, N1).transpose(0, 2, 1, 3)
    models = models.reshape(channels, N2 * row_local, N1)
    rows, feats, news, cols = [], [], [], []
    for q in range(channels):
        bands, feat = grid_channel(counts, lists, got, consts["forward"], q, tiles, owners)
        feats.append(feat)
        rows.append(exchange(bands))
    for q in range(channels):
        new, back = transform_channel(
            threshold, rows[q].reshape(owners * tiles * 16, LANES), models[q], consts, q, row_local
        )
        news.append(new)
        cols.append(exchange(back.reshape(owners, tiles, 2, 8, LANES)))
    returned = jnp.zeros((2 * senders, slots), F32)
    for q in range(channels):
        returned = degrid_channel(counts, lists, feats[q], cols[q], consts["backward"], returned, q)
    back = lax.all_to_all(
        returned.reshape(senders, 2, slots), ("fft", "chan"), split_axis=0, concat_axis=0, tiled=True
    )
    residuals = finish(visibilities[0], back.reshape(2 * senders, slots), send_counts)
    updated = jnp.stack(news).reshape(channels, N2, row_local, N1).transpose(0, 2, 1, 3)
    return (updated.reshape(model_image.shape), residuals[None])


def solution(mesh):
    placed = (
        P(("fft", "chan"), None, None, None),
        P(("fft", "chan"), None, None, None),
        P(("fft", "chan"), None, None),
        P(("fft", "chan"), None, None),
        P(("fft", "chan"), None, None),
        P(("fft", "chan"), None),
        P(("fft", "chan"), None, None),
        P(("fft", "chan"), None),
        P("chan", "fft", None),
        P("chan"),
    )
    return jax.shard_map(
        per_device,
        mesh=mesh,
        in_specs=placed,
        out_specs=(P("chan", "fft", None), P(("fft", "chan"), None, None, None)),
        check_vma=False,
    )
```

```python
import math

import jax
import jax.numpy as jnp
import numpy as np
from jax import lax
from jax.experimental import pallas as pl
from jax.experimental.pallas import tpu as pltpu
from jax.sharding import PartitionSpec as P

BU = 64
LOOP_GAIN = 0.7
N1 = 128
N2 = 256
CHUNK = 1536
LANES = 128
BLOCK = 16
F32 = jnp.float32
BF16 = jnp.bfloat16
GAUSS = -1.0 / 0.72
VMEM_BYTES = 60 * 1024 * 1024

NN = (((1,), (0,)), ((), ()))
NT = (((1,), (1,)), ((), ()))
TN = (((0,), (0,)), ((), ()))


def split(x):
    high = x.astype(BF16)
    low = (x - high.astype(F32)).astype(BF16)
    return high, low


def mm(a, b, dims):
    return lax.dot_general(a, b, dims, preferred_element_type=F32)


def mm3(a, b, dims):
    return mm(a[0], b[0], dims) + (mm(a[1], b[0], dims) + mm(a[0], b[1], dims))


def np_split(x):
    x = np.asarray(x, np.float32)
    high = x.astype(jnp.bfloat16)
    low = (x - high.astype(np.float32)).astype(jnp.bfloat16)
    return np.stack([high, low])


def angles(rows, cols, modulus):
    product = np.arange(rows, dtype=np.int64)[:, None] * np.arange(cols, dtype=np.int64)[None, :] % modulus
    return 2.0 * np.pi / modulus * product


def tables(facet_rows, row_local, grid_side, dirty_scale, back_scale):
    phase = (grid_side // 2 + np.arange(BU))[None, :] * np.arange(facet_rows)[:, None] % facet_rows
    theta = 2.0 * np.pi / facet_rows * phase
    c, s = np.cos(theta), np.sin(theta)
    owners = facet_rows // row_local
    forward = np.zeros((owners, 2, row_local, 2, BU))
    cc, ss = c.reshape(owners, row_local, BU), s.reshape(owners, row_local, BU)
    forward[:, 0, :, 0], forward[:, 0, :, 1] = cc, ss
    forward[:, 1, :, 0], forward[:, 1, :, 1] = -ss, cc
    forward = forward.reshape(2 * facet_rows, 2 * BU)
    backward = forward.T * back_scale
    forward = forward * dirty_scale
    a = angles(N1, N1, N1)
    c, s = np.cos(a), np.sin(a)
    lead = np.block([[c, -s], [s, c]])
    a = angles(N2, N2, N2)
    tail = np.concatenate([np.cos(a), np.sin(a)], axis=1)
    tail_back = np.concatenate([np.cos(a), np.sin(a)], axis=0)
    a = angles(N2, N1, N1 * N2)
    twist = np.stack([np.cos(a), np.sin(a)]).astype(np.float32)
    return {
        "forward": np_split(forward),
        "backward": np_split(backward),
        "lead": np_split(lead),
        "tail": np_split(tail),
        "tail_back": np_split(tail_back),
        "twist": twist,
    }


def bumps(cell, centre, half, scale, length):
    line = lax.broadcasted_iota(jnp.int32, (length, cell.shape[1]), 0).astype(F32)
    d = line - centre
    return jnp.where(jnp.abs(line - cell) <= half, jnp.exp(d * d * scale), 0.0)


def window(cell, fraction, half, scale):
    block = jnp.floor((cell - half) * (1.0 / BLOCK))
    near = cell - block * BLOCK
    wide = jnp.broadcast_to(block, (BLOCK, block.shape[1])).astype(BF16)
    return wide, bumps(near, near + fraction, half, scale, 2 * BLOCK)


def place_window(wide, fine, length):
    zero = jnp.zeros_like(fine[:BLOCK])
    out = []
    before = None
    for b in range(length // BLOCK):
        here = wide == b
        piece = zero if before is None else jnp.where(before, fine[BLOCK:], zero)
        out.append(jnp.where(here, fine[:BLOCK], piece))
        before = here
    return jnp.concatenate(out, axis=0)


def pack_body(vis, pos, row, col, cls, out):
    rows = row.shape[0]
    for part in range(2):
        out[pl.ds(part, rows, stride=8), :] = vis[part]
        out[pl.ds(2 + part, rows, stride=8), :] = pos[part]
    out[pl.ds(4, rows, stride=8), :] = row[...].astype(F32)
    out[pl.ds(5, rows, stride=8), :] = col[...].astype(F32)
    out[pl.ds(6, rows, stride=8), :] = cls[...].astype(F32)
    out[pl.ds(7, rows, stride=8), :] = jnp.zeros((rows, row.shape[1]), F32)


def pack(vis, pos, row, col, cls):
    return pl.pallas_call(
        pack_body,
        out_shape=jax.ShapeDtypeStruct((8 * row.shape[0], row.shape[1]), F32),
        name="pack",
    )(vis, pos, row, col, cls)


def grid_kernel_body(counts, lists, got, forward, out, feats, tab, *, base):
    r = pl.program_id(0)
    senders = got.shape[0] // 8
    slots = got.shape[1]

    @pl.when(r == 0)
    def _():
        half_n = senders // 2
        for side in range(2):
            spot = slice(side * slots, (side + 1) * slots)
            spot_low = slice((2 + side) * slots, (3 + side) * slots)

            def plane(k):
                return got[pl.ds(8 * side + k, half_n, stride=16), :]

            for k in range(4):
                high, low = split(plane(k))
                tab[k * half_n : (k + 1) * half_n, spot] = high
                tab[k * half_n : (k + 1) * half_n, spot_low] = low
            tab[4 * half_n :, spot] = ((plane(4) * 4.0 + plane(6)) * 256.0).astype(BF16)
            tab[4 * half_n :, spot_low] = plane(5).astype(BF16)

    count = counts[base + r]
    live_chunks = (count + (CHUNK - 1)) // CHUNK
    half_n = senders // 2
    line = lax.broadcasted_iota(jnp.int32, (half_n, CHUNK), 0)
    low_line = lax.broadcasted_iota(jnp.int32, (2 * slots, CHUNK), 0).astype(BF16)
    tick = lax.broadcasted_iota(jnp.int32, (1, CHUNK), 1)

    def step(j, acc):
        start = pl.multiple_of(j * CHUNK, CHUNK)
        slot = lists[:, pl.ds(start, CHUNK)]
        upper = lax.shift_right_logical(slot, 8)
        lower = lax.bitwise_and(slot, 255).astype(F32).astype(BF16)
        pick = jnp.where(low_line == lower, jnp.asarray(1.0, BF16), jnp.asarray(0.0, BF16))
        picks = jnp.concatenate([pick, pick], axis=0)
        found = mm(tab[...], picks, NN)
        mine = line == upper
        vals = [
            jnp.sum(jnp.where(mine, found[k * half_n : (k + 1) * half_n], 0.0), axis=0, keepdims=True)
            for k in range(5)
        ]
        live = (start + tick) < count
        code = vals[4].astype(jnp.int32)
        cell_col = lax.bitwise_and(code, 255).astype(F32)
        cell_row = lax.shift_right_logical(code, 10).astype(F32)
        half = lax.bitwise_and(lax.shift_right_logical(code, 8), 3).astype(F32) + 1.0
        scale = GAUSS / (half * half)
        vr = jnp.where(live, vals[0], 0.0)
        vi = jnp.where(live, vals[1], 0.0)
        zero = jnp.zeros_like(scale)
        feats[:, pl.ds(start, CHUNK)] = jnp.concatenate(
            [cell_row, vals[2], cell_col, vals[3], half, scale, zero, zero], axis=0
        )
        wide, fine = window(cell_row, vals[2], half, scale)
        weighted = jnp.concatenate(
            [place_window(wide, part, BU) for v in (vr, vi) for part in split(fine * v)], axis=0
        )
        wide, fine = window(cell_col, vals[3], half, scale)
        ch, cl = [place_window(wide, part, N2) for part in split(fine)]
        both = mm(weighted, ch, NT)
        weighted_high = jnp.concatenate([weighted[:BU], weighted[2 * BU : 3 * BU]], axis=0)
        cross = mm(weighted_high, cl, NT)
        top = both[:BU] + (both[BU : 2 * BU] + cross[:BU])
        bottom = both[2 * BU : 3 * BU] + (both[3 * BU :] + cross[BU:])
        return acc + jnp.concatenate([top, bottom], axis=0)

    acc = lax.fori_loop(0, live_chunks, step, jnp.zeros((2 * BU, N2), F32))
    bands = mm3((forward[0], forward[1]), split(acc), NN)
    for h in range(2):
        out[:, h] = bands[:, h * LANES : (h + 1) * LANES].reshape(out.shape[0], 8, LANES)


def grid_channel(counts, lists, got, forward, channel, tiles, owners):
    local, cap = lists.shape
    base = channel * tiles
    spec = pltpu.PrefetchScalarGridSpec(
        num_scalar_prefetch=1,
        grid=(tiles,),
        in_specs=[
            pl.BlockSpec((None, 1, cap), lambda r, c: (base + r, 0, 0)),
            pl.BlockSpec(got.shape, lambda r, c: (0, 0)),
            pl.BlockSpec(forward.shape, lambda r, c: (0, 0, 0)),
        ],
        out_specs=[
            pl.BlockSpec((owners, None, 2, 8, LANES), lambda r, c: (0, r, 0, 0, 0)),
            pl.BlockSpec((None, 8, cap), lambda r, c: (r, 0, 0)),
        ],
        scratch_shapes=[pltpu.VMEM((5 * got.shape[0] // 16, 4 * got.shape[1]), BF16)],
    )

    def body(*refs):
        grid_kernel_body(*refs, base=base)

    return pl.pallas_call(
        body,
        grid_spec=spec,
        out_shape=[
            jax.ShapeDtypeStruct((owners, tiles, 2, 8, LANES), F32),
            jax.ShapeDtypeStruct((tiles, 8, cap), F32),
        ],
        compiler_params=pltpu.CompilerParams(vmem_limit_bytes=VMEM_BYTES),
        name="grid_tiles",
    )(counts, lists.reshape(local, 1, cap), got, forward)


def transform_body(clip, got, model, lead, tail, tail_back, twist, updated, out, *, channel, rows):
    level = clip[channel]
    tc, ts = twist[0], twist[1]
    lead_parts = (lead[0], lead[1])
    for l in range(rows):
        parts = [
            jnp.concatenate([got[pl.ds(h * 8 + part * rows + l, N1, stride=16), :] for h in range(2)], axis=1)
            for part in range(2)
        ]
        x = jnp.concatenate(parts, axis=0)
        y = mm3(split(x), lead_parts, TN)
        yr, yi = y[:, :N1], y[:, N1:]
        turned = jnp.concatenate([yr * tc + yi * ts, yi * tc - yr * ts], axis=0)
        dirty = mm3((tail[0], tail[1]), split(turned), NN)
        prior = model[pl.ds(l, N2, stride=rows), :]
        new = prior + LOOP_GAIN * (dirty - jnp.clip(dirty, -level, level))
        updated[pl.ds(l, N2, stride=rows), :] = new
        a = mm3((tail_back[0], tail_back[1]), split(new), NN)
        ar, ai = a[:N2], a[N2:]
        turned = jnp.concatenate([ar * tc - ai * ts, ar * ts + ai * tc], axis=1)
        z = mm3(lead_parts, split(turned), NT)
        for part in range(2):
            for h in range(2):
                out[pl.ds(h * 8 + part * rows + l, N1, stride=16), :] = z[
                    part * N1 : (part + 1) * N1, h * LANES : (h + 1) * LANES
                ]


def transform_channel(clip, got, model, consts, channel, rows):
    def body(*refs):
        transform_body(*refs, channel=channel, rows=rows)

    whole = pl.BlockSpec(memory_space=pltpu.VMEM)
    return pl.pallas_call(
        body,
        in_specs=[pl.BlockSpec(memory_space=pltpu.SMEM)] + [whole] * 6,
        out_specs=[whole, whole],
        out_shape=[
            jax.ShapeDtypeStruct(model.shape, F32),
            jax.ShapeDtypeStruct(got.shape, F32),
        ],
        compiler_params=pltpu.CompilerParams(vmem_limit_bytes=VMEM_BYTES),
        name="transform",
    )(clip, got, model, consts["lead"], consts["tail"], consts["tail_back"], consts["twist"])


def degrid_body(counts, lists, feats, got, backward, prior, out, acc_ref, *, base):
    r = pl.program_id(0)
    senders = prior.shape[0] // 2
    slots = prior.shape[1]

    @pl.when(r == 0)
    def _():
        acc_ref[...] = jnp.zeros_like(acc_ref)

    count = counts[base + r]
    live_chunks = (count + (CHUNK - 1)) // CHUNK
    spot = lax.broadcasted_iota(jnp.int32, (senders, CHUNK), 0).astype(BF16)
    one, none = jnp.asarray(1.0, BF16), jnp.asarray(0.0, BF16)
    tick = lax.broadcasted_iota(jnp.int32, (1, CHUNK), 1)
    columns = jnp.concatenate([got[:, h].reshape(got.shape[0] * 8, LANES) for h in range(2)], axis=1)
    pred = mm3((backward[0], backward[1]), split(columns), NN)
    ph, pw = split(pred)

    def step(j, acc):
        start = pl.multiple_of(j * CHUNK, CHUNK)
        slot = lists[:, pl.ds(start, CHUNK)]
        sender = lax.shift_right_logical(slot, 7).astype(F32).astype(BF16)
        place = lax.bitwise_and(slot, slots - 1).astype(F32).astype(BF16)
        live = (start + tick) < count
        feat = feats[:, pl.ds(start, CHUNK)]
        half, scale = feat[4:5], feat[5:6]
        rows = bumps(feat[0:1], feat[0:1] + feat[1:2], half, scale, BU)
        wide, fine = window(feat[2:3], feat[3:4], half, scale)
        ch, cl = [place_window(wide, part, N2) for part in split(fine)]
        both = mm(jnp.concatenate([ph, pw], axis=0), ch, NN)
        t = both[: 2 * BU] + (both[2 * BU :] + mm(ph, cl, NN))
        pick = jnp.where(spot == place, one, none)
        mine = spot == sender
        sides = []
        for part in range(2):
            val = jnp.sum(t[part * BU : (part + 1) * BU] * rows, axis=0, keepdims=True)
            val = jnp.where(live, val, 0.0)
            for piece in split(val):
                sides.append(jnp.where(mine, piece, none))
        spread = mm(jnp.concatenate(sides, axis=0), pick, NT)
        return acc + spread

    acc_ref[...] = lax.fori_loop(0, live_chunks, step, acc_ref[...])

    @pl.when(r == pl.num_programs(0) - 1)
    def _():
        for part in range(2):
            lo = 2 * part * senders
            total = acc_ref[lo : lo + senders] + acc_ref[lo + senders : lo + 2 * senders]
            out[pl.ds(part, senders, stride=2), :] = prior[pl.ds(part, senders, stride=2), :] + total


def degrid_channel(counts, lists, feats, got, backward, prior, channel):
    owners, tiles = got.shape[:2]
    local, cap = lists.shape
    base = channel * tiles
    spec = pltpu.PrefetchScalarGridSpec(
        num_scalar_prefetch=1,
        grid=(tiles,),
        in_specs=[
            pl.BlockSpec((None, 1, cap), lambda r, c: (base + r, 0, 0)),
            pl.BlockSpec((None, 8, cap), lambda r, c: (r, 0, 0)),
            pl.BlockSpec((owners, None, 2, 8, LANES), lambda r, c: (0, r, 0, 0, 0)),
            pl.BlockSpec(backward.shape, lambda r, c: (0, 0, 0)),
            pl.BlockSpec(prior.shape, lambda r, c: (0, 0)),
        ],
        out_specs=pl.BlockSpec(prior.shape, lambda r, c: (0, 0)),
        scratch_shapes=[pltpu.VMEM((2 * prior.shape[0], prior.shape[1]), F32)],
    )

    def body(*refs):
        degrid_body(*refs, base=base)

    return pl.pallas_call(
        body,
        grid_spec=spec,
        out_shape=jax.ShapeDtypeStruct(prior.shape, F32),
        compiler_params=pltpu.CompilerParams(vmem_limit_bytes=VMEM_BYTES),
        name="degrid_tiles",
    )(counts, lists.reshape(local, 1, cap), feats, got, backward, prior)


def finish_body(vis, got, counts, out):
    rows, slots = got.shape[0] // 2, got.shape[1]
    limit = jnp.broadcast_to(counts[...], (rows, rows)).T[:, :slots]
    lane = lax.broadcasted_iota(jnp.int32, (rows, slots), 1)
    for part in range(2):
        diff = vis[part] - got[pl.ds(part, rows, stride=2), :]
        out[part] = jnp.where(lane < limit, diff, 0.0)


def finish(vis, got, counts):
    return pl.pallas_call(
        finish_body,
        out_shape=jax.ShapeDtypeStruct(vis.shape, F32),
        name="finish",
    )(vis, got, counts)


def per_device(
    visibilities,
    positions,
    cell_row,
    cell_column,
    kernel_class,
    send_counts,
    tile_lists,
    tile_counts,
    model_image,
    threshold,
):
    owners = lax.axis_size("fft")
    senders = owners * lax.axis_size("chan")
    slots = visibilities.shape[3]
    channels, row_local, grid_side = model_image.shape
    cap = tile_lists.shape[2]
    tiles = tile_lists.shape[1] // channels
    facet_rows = row_local * owners
    dirty_scale = 1.0 / math.sqrt(owners * tiles * cap)
    back_scale = 0.5 / math.sqrt(facet_rows * grid_side)
    consts = {k: jnp.asarray(v) for k, v in tables(facet_rows, row_local, grid_side, dirty_scale, back_scale).items()}
    lists, counts = tile_lists[0], tile_counts[0]

    payload = pack(visibilities[0], positions[0], cell_row[0], cell_column[0], kernel_class[0])
    got = lax.all_to_all(
        payload.reshape(senders, 8, slots), ("fft", "chan"), split_axis=0, concat_axis=0, tiled=True
    ).reshape(8 * senders, slots)

    def exchange(x):
        return lax.all_to_all(x, "fft", split_axis=0, concat_axis=0, tiled=True)

    models = model_image.reshape(channels, row_local, N2, N1).transpose(0, 2, 1, 3)
    models = models.reshape(channels, N2 * row_local, N1)
    rows, feats, news, cols = [], [], [], []
    for q in range(channels):
        bands, feat = grid_channel(counts, lists, got, consts["forward"], q, tiles, owners)
        feats.append(feat)
        rows.append(exchange(bands))
    for q in range(channels):
        new, back = transform_channel(
            threshold, rows[q].reshape(owners * tiles * 16, LANES), models[q], consts, q, row_local
        )
        news.append(new)
        cols.append(exchange(back.reshape(owners, tiles, 2, 8, LANES)))
    returned = jnp.zeros((2 * senders, slots), F32)
    for q in range(channels):
        returned = degrid_channel(counts, lists, feats[q], cols[q], consts["backward"], returned, q)
    back = lax.all_to_all(
        returned.reshape(senders, 2, slots), ("fft", "chan"), split_axis=0, concat_axis=0, tiled=True
    )
    residuals = finish(visibilities[0], back.reshape(2 * senders, slots), send_counts)
    updated = jnp.stack(news).reshape(channels, N2, row_local, N1).transpose(0, 2, 1, 3)
    return (updated.reshape(model_image.shape), residuals[None])


def solution(mesh):
    placed = (
        P(("fft", "chan"), None, None, None),
        P(("fft", "chan"), None, None, None),
        P(("fft", "chan"), None, None),
        P(("fft", "chan"), None, None),
        P(("fft", "chan"), None, None),
        P(("fft", "chan"), None),
        P(("fft", "chan"), None, None),
        P(("fft", "chan"), None),
        P("chan", "fft", None),
        P("chan"),
    )
    return jax.shard_map(
        per_device,
        mesh=mesh,
        in_specs=placed,
        out_specs=(P("chan", "fft", None), P(("fft", "chan"), None, None, None)),
        check_vma=False,
    )
```

```python
import math

import jax
import jax.numpy as jnp
import numpy as np
from jax import lax
from jax.experimental import pallas as pl
from jax.experimental.pallas import tpu as pltpu
from jax.sharding import PartitionSpec as P

BU = 64
LOOP_GAIN = 0.7
N1 = 128
N2 = 256
LANES = 128
BLOCK = 16
F32 = jnp.float32
BF16 = jnp.bfloat16
GAUSS = -1.0 / 0.72
VMEM_BYTES = 60 * 1024 * 1024

NN = (((1,), (0,)), ((), ()))
NT = (((1,), (1,)), ((), ()))


def split(x):
    high = x.astype(BF16)
    low = (x - high.astype(F32)).astype(BF16)
    return high, low


def mm(a, b, dims):
    return lax.dot_general(a, b, dims, preferred_element_type=F32)


def mm3(a, b, dims):
    return mm(a[0], b[0], dims) + (mm(a[1], b[0], dims) + mm(a[0], b[1], dims))


def np_split(x):
    x = np.asarray(x, np.float32)
    high = x.astype(jnp.bfloat16)
    low = (x - high.astype(np.float32)).astype(jnp.bfloat16)
    return np.stack([high, low])


def angles(rows, cols, modulus):
    product = np.arange(rows, dtype=np.int64)[:, None] * np.arange(cols, dtype=np.int64)[None, :] % modulus
    return 2.0 * np.pi / modulus * product


def tables(facet_rows, row_local, grid_side, dirty_scale, back_scale):
    phase = (grid_side // 2 + np.arange(BU))[None, :] * np.arange(facet_rows)[:, None] % facet_rows
    theta = 2.0 * np.pi / facet_rows * phase
    c, s = np.cos(theta), np.sin(theta)
    owners = facet_rows // row_local
    direct = np.zeros((owners, 2, row_local, 2, BU))
    cc, ss = c.reshape(owners, row_local, BU), s.reshape(owners, row_local, BU)
    direct[:, 0, :, 0], direct[:, 0, :, 1] = cc, ss
    direct[:, 1, :, 0], direct[:, 1, :, 1] = -ss, cc
    mirror = direct.copy()
    mirror[:, 1] *= -1.0
    shape = (2 * facet_rows, 2 * BU)
    bands = np.concatenate([direct.reshape(shape), mirror.reshape(shape)], axis=1)
    a = angles(N1, N1 // 2, N1)
    c, s = np.cos(a), np.sin(a)
    lead = np.block([[c, s], [-s, c]])
    a = angles(N2, N2, N2)
    tail = np.stack([np.cos(a), np.sin(a)])
    a = angles(N1, N2, N1 * N2)
    twist = np.stack([np.cos(a), np.sin(a)]).astype(np.float32)
    return {
        "forward": np_split(bands * dirty_scale),
        "backward": np_split(bands.T * back_scale),
        "lead": np_split(lead),
        "lead_back": np_split(lead.T),
        "tail": np_split(tail),
        "twist": twist,
        "twist_back": twist.transpose(0, 2, 1).copy(),
    }


def bumps(cell, centre, half, scale, length):
    line = lax.broadcasted_iota(jnp.int32, (length, cell.shape[1]), 0).astype(F32)
    d = line - centre
    return jnp.where(jnp.abs(line - cell) <= half, jnp.exp(d * d * scale), 0.0)


def window(cell, fraction, half, scale):
    block = jnp.floor((cell - half) * (1.0 / BLOCK))
    near = cell - block * BLOCK
    wide = jnp.broadcast_to(block, (BLOCK, block.shape[1])).astype(BF16)
    return wide, bumps(near, near + fraction, half, scale, 2 * BLOCK)


def place_window(wide, fine, length):
    zero = jnp.zeros_like(fine[:BLOCK])
    out = []
    before = None
    for b in range(length // BLOCK):
        here = wide == b
        piece = zero if before is None else jnp.where(before, fine[BLOCK:], zero)
        out.append(jnp.where(here, fine[:BLOCK], piece))
        before = here
    return jnp.concatenate(out, axis=0)


def pack_body(vis, pos, row, col, cls, out):
    rows = row.shape[0]
    for part in range(2):
        out[pl.ds(part, rows, stride=8), :] = vis[part]
        out[pl.ds(2 + part, rows, stride=8), :] = pos[part]
    out[pl.ds(4, rows, stride=8), :] = row[...].astype(F32)
    out[pl.ds(5, rows, stride=8), :] = col[...].astype(F32)
    out[pl.ds(6, rows, stride=8), :] = cls[...].astype(F32)
    out[pl.ds(7, rows, stride=8), :] = jnp.zeros((rows, row.shape[1]), F32)


def pack(vis, pos, row, col, cls):
    return pl.pallas_call(
        pack_body,
        out_shape=jax.ShapeDtypeStruct((8 * row.shape[0], row.shape[1]), F32),
        name="pack",
    )(vis, pos, row, col, cls)


def build_table(got, tab):
    senders = got.shape[0] // 8
    slots = got.shape[1]
    half_n = senders // 2
    for side in range(2):
        spot = slice(side * slots, (side + 1) * slots)
        spot_low = slice((2 + side) * slots, (3 + side) * slots)

        def plane(k):
            return got[pl.ds(8 * side + k, half_n, stride=16), :]

        for k in range(4):
            high, low = split(plane(k))
            tab[k * half_n : (k + 1) * half_n, spot] = high
            tab[k * half_n : (k + 1) * half_n, spot_low] = low
        tab[4 * half_n :, spot] = ((plane(4) * 4.0 + plane(6)) * 256.0).astype(BF16)
        tab[4 * half_n :, spot_low] = plane(5).astype(BF16)


def gather_list(slot, tab):
    cap = slot.shape[1]
    half_n = tab.shape[0] // 5
    places = tab.shape[1] // 2
    line = lax.broadcasted_iota(jnp.int32, (half_n, cap), 0)
    low_line = lax.broadcasted_iota(jnp.int32, (places, cap), 0).astype(BF16)
    upper = lax.shift_right_logical(slot, 8)
    lower = lax.bitwise_and(slot, 255).astype(F32).astype(BF16)
    pick = jnp.where(low_line == lower, jnp.asarray(1.0, BF16), jnp.asarray(0.0, BF16))
    found = mm(tab[...], jnp.concatenate([pick, pick], axis=0), NN)
    mine = line == upper
    vals = [
        jnp.sum(jnp.where(mine, found[k * half_n : (k + 1) * half_n], 0.0), axis=0, keepdims=True) for k in range(5)
    ]
    code = vals[4].astype(jnp.int32)
    cell_col = lax.bitwise_and(code, 255).astype(F32)
    cell_row = lax.shift_right_logical(code, 10).astype(F32)
    half = lax.bitwise_and(lax.shift_right_logical(code, 8), 3).astype(F32) + 1.0
    zero = jnp.zeros_like(half)
    return jnp.concatenate([cell_row, vals[2], cell_col, vals[3], half, vals[0], vals[1], zero], axis=0)


def oriented(feat, flip):
    sign = 1.0 - 2.0 * flip.astype(F32)
    shift = flip.astype(F32) * N2
    half = feat[4:5]
    return feat[2:3] * sign + shift, feat[3:4] * sign, half, GAUSS / (half * half)


def grid_list(feat, flip):
    cell_col, offset, half, scale = oriented(feat, flip)
    wide, fine = window(feat[0:1], feat[1:2], half, scale)
    parts = [split(fine * feat[k : k + 1]) for k in (5, 6)]
    weighted = jnp.concatenate(
        [place_window(wide, parts[part][piece], BU) for piece in range(2) for part in range(2)], axis=0
    )
    wide, fine = window(cell_col, offset, half, scale)
    ch, cl = [place_window(wide, piece, N2 + BLOCK) for piece in split(fine)]
    both = mm(ch, weighted, NT)
    cross = mm(cl, weighted[: 2 * BU], NT)
    return both[:, : 2 * BU] + (both[:, 2 * BU :] + cross)


def gather_body(meta, lists, got, feats, tab):
    @pl.when(pl.program_id(0) == 0)
    def _():
        build_table(got, tab)

    feats[...] = gather_list(lists[...], tab)


def own_body(meta, lists, got, feats, acc, tab):
    @pl.when(pl.program_id(0) == 0)
    def _():
        build_table(got, tab)

    feat = gather_list(lists[...], tab)
    feats[...] = feat
    acc[...] = grid_list(feat, meta[0])


def own_tile(r, high):
    return r + high * (3 - 2 * r)


def guest_tile(r, high):
    return own_tile(r, 1 - high)


def gather_lists(meta, lists, got, tiles):
    cap = lists.shape[2]
    spec = pltpu.PrefetchScalarGridSpec(
        num_scalar_prefetch=1,
        grid=(tiles,),
        in_specs=[
            pl.BlockSpec((None, 1, cap), lambda r, m: ((1 - m[0]) * tiles + r, 0, 0)),
            pl.BlockSpec(got.shape, lambda r, m: (0, 0)),
        ],
        out_specs=pl.BlockSpec((None, 8, cap), lambda r, m: (r, 0, 0)),
        scratch_shapes=[pltpu.VMEM((5 * got.shape[0] // 16, 4 * got.shape[1]), BF16)],
    )
    return pl.pallas_call(
        gather_body,
        grid_spec=spec,
        out_shape=jax.ShapeDtypeStruct((tiles, 8, cap), F32),
        compiler_params=pltpu.CompilerParams(vmem_limit_bytes=VMEM_BYTES),
        name="gather_lists",
    )(meta, lists, got)


def grid_own(meta, lists, got, tiles):
    cap = lists.shape[2]
    spec = pltpu.PrefetchScalarGridSpec(
        num_scalar_prefetch=1,
        grid=(tiles,),
        in_specs=[
            pl.BlockSpec((None, 1, cap), lambda r, m: (m[0] * tiles + own_tile(r, m[0]), 0, 0)),
            pl.BlockSpec(got.shape, lambda r, m: (0, 0)),
        ],
        out_specs=[
            pl.BlockSpec((None, 8, cap), lambda r, m: (r, 0, 0)),
            pl.BlockSpec((None, N2 + BLOCK, 2 * BU), lambda r, m: (r, 0, 0)),
        ],
        scratch_shapes=[pltpu.VMEM((5 * got.shape[0] // 16, 4 * got.shape[1]), BF16)],
    )
    return pl.pallas_call(
        own_body,
        grid_spec=spec,
        out_shape=[
            jax.ShapeDtypeStruct((tiles, 8, cap), F32),
            jax.ShapeDtypeStruct((tiles, N2 + BLOCK, 2 * BU), F32),
        ],
        compiler_params=pltpu.CompilerParams(vmem_limit_bytes=VMEM_BYTES),
        name="grid_own",
    )(meta, lists, got)


def guest_body(meta, feats, own, forward, out, carry):
    r = pl.program_id(0)
    high = meta[0]
    owners = out.shape[0]

    @pl.when(r == 0)
    def _():
        carry[...] = jnp.zeros_like(carry)

    guest = grid_list(feats[...], 1 - high)
    mine = own[...]
    swap = high == 1
    acc = jnp.concatenate([jnp.where(swap, guest, mine), jnp.where(swap, mine, guest)], axis=1)
    acc = jnp.concatenate([acc[:BLOCK] + carry[...], acc[BLOCK:N2]], axis=0), acc[N2:]
    carry[...] = acc[1]
    table = (forward[0], forward[1])
    bands = mm3(table, split(acc[0]), NT)
    for h in range(2):
        out[:, pl.ds(2 * r + h, 1)] = bands[:, h * LANES : (h + 1) * LANES].reshape(owners, 1, 8, LANES)

    @pl.when(r == pl.num_programs(0) - 1)
    def _():
        edge = mm3(table, split(acc[1]), NT)
        edge = jnp.concatenate([edge, jnp.zeros((edge.shape[0], LANES - BLOCK), F32)], axis=1)
        out[:, 8:9] = edge.reshape(owners, 1, 8, LANES)


def grid_guest(meta, feats, own, forward, owners):
    tiles, _, cap = feats.shape
    shape = (owners, 2 * tiles + 1, 8, LANES)
    spec = pltpu.PrefetchScalarGridSpec(
        num_scalar_prefetch=1,
        grid=(tiles,),
        in_specs=[
            pl.BlockSpec((None, 8, cap), lambda r, m: (guest_tile(r, m[0]), 0, 0)),
            pl.BlockSpec((None,) + own.shape[1:], lambda r, m: (r, 0, 0)),
            pl.BlockSpec(forward.shape, lambda r, m: (0, 0, 0)),
        ],
        out_specs=pl.BlockSpec(shape, lambda r, m: (0, 0, 0, 0)),
        scratch_shapes=[pltpu.VMEM((BLOCK, 4 * BU), F32)],
    )
    return pl.pallas_call(
        guest_body,
        grid_spec=spec,
        out_shape=jax.ShapeDtypeStruct(shape, F32),
        compiler_params=pltpu.CompilerParams(vmem_limit_bytes=VMEM_BYTES),
        name="grid_guest",
    )(meta, feats, own, forward)


def transform_body(clip, got, model, lead, lead_back, tail, twist, twist_back, updated, out, xs, zs, *, rows):
    pairs = xs.shape[0] // 128
    owners = 2 * pairs
    half_n = N1 // 2
    span = pairs * 64
    plane = model.shape[0] // 2
    tc, ts = twist[0], twist[1]
    bc, bs = twist_back[0], twist_back[1]
    lead_parts = (lead[0], lead[1])
    back_parts = (lead_back[0], lead_back[1])
    wide = [jnp.concatenate([tail[p, 0], tail[p, 1]], axis=1) for p in range(2)]
    tall = [jnp.concatenate([tail[p, 0], tail[p, 1]], axis=0) for p in range(2)]
    lane = lax.broadcasted_iota(jnp.int32, (1, N1), 1)
    flip = jnp.where(lax.bitwise_and(lane, 1) == 0, 1.0, -1.0)
    row_id = lax.broadcasted_iota(jnp.int32, (8, LANES), 0)

    def place(q, g):
        return g if q == 0 else owners - 1 - g

    for q in range(2):
        for g in range(pairs):
            src = place(q, g) * 72
            dst = q * span + g * 64
            first = got[src : src + 8, :]
            if g > 0:
                past = place(q, g - 1) * 72 + 64
                first = first + got[past : past + 8, :]
            xs[dst : dst + 8, :] = first
            xs[dst + 8 : dst + 64, :] = got[src + 8 : src + 64, :]
    for q in range(2):
        level = clip[q]
        middle = place(q, pairs - 1) * 72 + 64
        edge = jnp.zeros((8, LANES), F32)
        for l in range(0, rows, 2):
            turned = []
            for k in range(2):
                parts = [
                    jnp.concatenate(
                        [xs[pl.ds(q * span + h * 8 + part * rows + l + k, half_n, stride=16), :] for h in range(2)],
                        axis=1,
                    )
                    for part in range(2)
                ]
                y = mm3(lead_parts, split(jnp.concatenate(parts, axis=0)), NN)
                yr, yi = y[:N1], y[N1:]
                turned.append(jnp.concatenate([yr * tc + yi * ts, yi * tc - yr * ts], axis=1))
            dirty = mm3(wide, split(jnp.concatenate(turned, axis=0)), NT)
            news = []
            for k in range(2):
                part = dirty[:, k * N1 : (k + 1) * N1] + flip * got[middle + l + k : middle + l + k + 1, 0:1]
                prior = model[pl.ds(q * plane + l + k, N2, stride=rows), :]
                new = prior + LOOP_GAIN * (part - jnp.clip(part, -level, level))
                updated[pl.ds(q * plane + l + k, N2, stride=rows), :] = new
                news.append(new)
            a = mm3(tall, split(jnp.concatenate(news, axis=1)), NN)
            for k in range(2):
                ar, ai = a[:N2, k * N1 : (k + 1) * N1], a[N2:, k * N1 : (k + 1) * N1]
                last = jnp.sum(ar[0:1] * flip, axis=1, keepdims=True)
                edge = jnp.where(row_id == l + k, last, edge)
                back = jnp.concatenate([ar * bc - ai * bs, ar * bs + ai * bc], axis=1)
                z = mm3(back_parts, split(back), NT)
                for part in range(2):
                    for h in range(2):
                        zs[pl.ds(q * span + h * 8 + part * rows + l + k, half_n, stride=16), :] = z[
                            part * half_n : (part + 1) * half_n, h * LANES : (h + 1) * LANES
                        ]
        for g in range(pairs):
            src = q * span + g * 64
            dst = place(q, g) * 72
            out[dst : dst + 64, :] = zs[src : src + 64, :]
            out[dst + 64 : dst + 72, :] = zs[src + 64 : src + 72, :] if g + 1 < pairs else edge


def transform(clip, got, model, consts, rows, owners):
    def body(*refs):
        transform_body(*refs, rows=rows)

    whole = pl.BlockSpec(memory_space=pltpu.VMEM)
    span = owners // 2 * 64
    return pl.pallas_call(
        body,
        in_specs=[pl.BlockSpec(memory_space=pltpu.SMEM)] + [whole] * 7,
        out_specs=[whole, whole],
        out_shape=[
            jax.ShapeDtypeStruct(model.shape, F32),
            jax.ShapeDtypeStruct(got.shape, F32),
        ],
        scratch_shapes=[pltpu.VMEM((2 * span, LANES), F32), pltpu.VMEM((2 * span, LANES), F32)],
        compiler_params=pltpu.CompilerParams(vmem_limit_bytes=VMEM_BYTES),
        name="transform",
    )(
        clip, got, model, consts["lead"], consts["lead_back"], consts["tail"], consts["twist"], consts["twist_back"]
    )


def degrid_body(meta, lists, guest_lists, feats, guest_feats, got, backward, out, acc_ref):
    r = pl.program_id(0)
    high = meta[0]
    slots = out.shape[1]
    senders = out.shape[0] // 4
    cap = lists.shape[1]

    spot = lax.broadcasted_iota(jnp.int32, (senders, cap), 0).astype(BF16)
    one, none = jnp.asarray(1.0, BF16), jnp.asarray(0.0, BF16)
    owners = got.shape[0]
    columns = jnp.concatenate([got[:, pl.ds(2 * r + h, 1)].reshape(owners * 8, LANES) for h in range(3)], axis=1)
    pred = mm3((backward[0], backward[1]), split(columns), NN)
    swap = high == 1
    direct, mirror = pred[: 2 * BU], pred[2 * BU :]
    sources = (
        (lists, feats, jnp.where(swap, mirror, direct), high),
        (guest_lists, guest_feats, jnp.where(swap, direct, mirror), 1 - high),
    )
    for which, (list_ref, feat_ref, mine_pred, turn) in enumerate(sources):
        slot = list_ref[...]
        sender = lax.shift_right_logical(slot, 7).astype(F32).astype(BF16)
        place = lax.bitwise_and(slot, slots - 1).astype(F32).astype(BF16)
        feat = feat_ref[...]
        cell_col, offset, half, scale = oriented(feat, turn)
        rows = bumps(feat[0:1], feat[0:1] + feat[1:2], half, scale, BU)
        wide, fine = window(cell_col, offset, half, scale)
        ch, cl = [place_window(wide, piece, N2) for piece in split(fine)]
        ph, pw = split(mine_pred[:, :N2])
        both = mm(jnp.concatenate([ph, pw], axis=0), ch, NN)
        t = both[: 2 * BU] + (both[2 * BU :] + mm(ph, cl, NN))
        gap = N2 - cell_col
        past = gap - offset
        rim = jnp.where(jnp.abs(gap) <= half, jnp.exp(past * past * scale), 0.0)
        t = t + mine_pred[:, N2 : N2 + 1] * rim
        pick = jnp.where(spot == place, one, none)
        mine = spot == sender
        sides = []
        for part in range(2):
            val = jnp.sum(t[part * BU : (part + 1) * BU] * rows, axis=0, keepdims=True)
            for piece in split(val):
                sides.append(jnp.where(mine, piece, none))
        spread = mm(jnp.concatenate(sides, axis=0), pick, NT)
        acc_ref[which] = jnp.where(r == 0, 0.0, acc_ref[which]) + spread

    @pl.when(r == pl.num_programs(0) - 1)
    def _():
        for which in range(2):
            for part in range(2):
                lo = 2 * part * senders
                total = acc_ref[which, lo : lo + senders] + acc_ref[which, lo + senders : lo + 2 * senders]
                out[pl.ds(2 * which + part, senders, stride=4), :] = total


def degrid(meta, lists, guest_lists, feats, guest_feats, got, backward, senders, slots):
    tiles, _, cap = feats.shape
    spec = pltpu.PrefetchScalarGridSpec(
        num_scalar_prefetch=1,
        grid=(tiles,),
        in_specs=[
            pl.BlockSpec((None, 1, cap), lambda r, m: (m[0] * tiles + own_tile(r, m[0]), 0, 0)),
            pl.BlockSpec((None, 1, cap), lambda r, m: (m[0] * tiles + guest_tile(r, m[0]), 0, 0)),
            pl.BlockSpec((None, 8, cap), lambda r, m: (r, 0, 0)),
            pl.BlockSpec((None, 8, cap), lambda r, m: (guest_tile(r, m[0]), 0, 0)),
            pl.BlockSpec(got.shape, lambda r, m: (0, 0, 0, 0)),
            pl.BlockSpec(backward.shape, lambda r, m: (0, 0, 0)),
        ],
        out_specs=pl.BlockSpec((4 * senders, slots), lambda r, m: (0, 0)),
        scratch_shapes=[pltpu.VMEM((2, 4 * senders, slots), F32)],
    )
    return pl.pallas_call(
        degrid_body,
        grid_spec=spec,
        out_shape=jax.ShapeDtypeStruct((4 * senders, slots), F32),
        compiler_params=pltpu.CompilerParams(vmem_limit_bytes=VMEM_BYTES),
        name="degrid_tiles",
    )(meta, lists, guest_lists, feats, guest_feats, got, backward)


def finish_body(vis, got, counts, out, turned, *, group):
    rows, slots = got.shape[0] // 4, got.shape[1]
    owners = rows // group
    step = 4 * group
    for f in range(owners):
        lo = (owners - 1 - f) * step
        turned[f * step : (f + 1) * step, :] = got[lo : lo + step, :]
    limit = jnp.broadcast_to(counts[...], (rows, rows)).T[:, :slots]
    lane = lax.broadcasted_iota(jnp.int32, (rows, slots), 1)
    for part in range(2):
        back = got[pl.ds(part, rows, stride=4), :] + turned[pl.ds(2 + part, rows, stride=4), :]
        out[part] = jnp.where(lane < limit, vis[part] - back, 0.0)


def finish(vis, got, counts, group):
    def body(*refs):
        finish_body(*refs, group=group)

    return pl.pallas_call(
        body,
        out_shape=jax.ShapeDtypeStruct(vis.shape, F32),
        scratch_shapes=[pltpu.VMEM(got.shape, F32)],
        name="finish",
    )(vis, got, counts)


def per_device(
    visibilities,
    positions,
    cell_row,
    cell_column,
    kernel_class,
    send_counts,
    tile_lists,
    tile_counts,
    model_image,
    threshold,
):
    owners = lax.axis_size("fft")
    group = lax.axis_size("chan")
    senders = owners * group
    slots = visibilities.shape[3]
    channels, row_local, grid_side = model_image.shape
    cap = tile_lists.shape[2]
    tiles = tile_lists.shape[1] // channels
    facet_rows = row_local * owners
    dirty_scale = 1.0 / math.sqrt(owners * tiles * cap)
    back_scale = 0.5 / math.sqrt(facet_rows * grid_side)
    consts = {k: jnp.asarray(v) for k, v in tables(facet_rows, row_local, grid_side, dirty_scale, back_scale).items()}
    swap = [(i, owners - 1 - i) for i in range(owners)]
    meta = (lax.axis_index("fft") >= owners // 2).astype(jnp.int32).reshape(1)
    live = jnp.arange(cap, dtype=jnp.int32)[None, :] < tile_counts[0][:, None]
    lists = jnp.where(live, tile_lists[0], senders * slots)[:, None, :]

    payload = pack(visibilities[0], positions[0], cell_row[0], cell_column[0], kernel_class[0])
    got = lax.all_to_all(
        payload.reshape(senders, 8, slots), ("fft", "chan"), split_axis=0, concat_axis=0, tiled=True
    ).reshape(8 * senders, slots)
    guest_lists = lax.ppermute(lists, "fft", swap)

    def exchange(x):
        return lax.all_to_all(x, "fft", split_axis=0, concat_axis=0, tiled=True)

    guest_feats = lax.ppermute(gather_lists(meta, lists, got, tiles), "fft", swap)
    feats, own = grid_own(meta, lists, got, tiles)
    rows = exchange(grid_guest(meta, guest_feats, own, consts["forward"], owners))
    blocks = 2 * tiles + 1
    models = model_image.reshape(channels, row_local, N2, N1).transpose(0, 2, 1, 3)
    models = models.reshape(channels * N2 * row_local, N1)
    updated, back = transform(threshold, rows.reshape(owners * blocks * 8, LANES), models, consts, row_local, owners)
    cols = exchange(back.reshape(owners, blocks, 8, LANES))
    returned = degrid(meta, lists, guest_lists, feats, guest_feats, cols, consts["backward"], senders, slots)
    back = lax.all_to_all(
        returned.reshape(senders, 4, slots), ("fft", "chan"), split_axis=0, concat_axis=0, tiled=True
    )
    residuals = finish(visibilities[0], back.reshape(4 * senders, slots), send_counts, group)
    updated = updated.reshape(channels, N2, row_local, N1).transpose(0, 2, 1, 3)
    return (updated.reshape(model_image.shape), residuals[None])


def solution(mesh):
    placed = (
        P(("fft", "chan"), None, None, None),
        P(("fft", "chan"), None, None, None),
        P(("fft", "chan"), None, None),
        P(("fft", "chan"), None, None),
        P(("fft", "chan"), None, None),
        P(("fft", "chan"), None),
        P(("fft", "chan"), None, None),
        P(("fft", "chan"), None),
        P("chan", "fft", None),
        P("chan"),
    )
    return jax.shard_map(
        per_device,
        mesh=mesh,
        in_specs=placed,
        out_specs=(P("chan", "fft", None), P(("fft", "chan"), None, None, None)),
        check_vma=False,
    )
```

```python
import math

import jax
import jax.numpy as jnp
import numpy as np
from jax import lax
from jax.experimental import pallas as pl
from jax.experimental.pallas import tpu as pltpu
from jax.sharding import PartitionSpec as P

BU = 64
LOOP_GAIN = 0.7
N1 = 128
N2 = 256
LANES = 128
BLOCK = 16
F32 = jnp.float32
BF16 = jnp.bfloat16
GAUSS = -1.0 / 0.72
VMEM_BYTES = 60 * 1024 * 1024

NN = (((1,), (0,)), ((), ()))
NT = (((1,), (1,)), ((), ()))


def split(x):
    high = x.astype(BF16)
    low = (x - high.astype(F32)).astype(BF16)
    return high, low


def mm(a, b, dims):
    return lax.dot_general(a, b, dims, preferred_element_type=F32)


def mm3(table, b, dims):
    m = table.shape[0] // 2
    high, low = split(b)
    both = mm(table, high, dims)
    return both[:m] + (both[m:] + mm(table[:m], low, dims))


def np_split(x):
    x = np.asarray(x, np.float32)
    high = x.astype(jnp.bfloat16)
    low = (x - high.astype(np.float32)).astype(jnp.bfloat16)
    return np.concatenate([high, low], axis=-2)


def angles(rows, cols, modulus):
    product = np.arange(rows, dtype=np.int64)[:, None] * np.arange(cols, dtype=np.int64)[None, :] % modulus
    return 2.0 * np.pi / modulus * product


def tables(facet_rows, row_local, grid_side, dirty_scale, back_scale):
    phase = (grid_side // 2 + np.arange(BU))[None, :] * np.arange(facet_rows)[:, None] % facet_rows
    theta = 2.0 * np.pi / facet_rows * phase
    c, s = np.cos(theta), np.sin(theta)
    owners = facet_rows // row_local
    direct = np.zeros((owners, 2, row_local, 2, BU))
    cc, ss = c.reshape(owners, row_local, BU), s.reshape(owners, row_local, BU)
    direct[:, 0, :, 0], direct[:, 0, :, 1] = cc, ss
    direct[:, 1, :, 0], direct[:, 1, :, 1] = -ss, cc
    mirror = direct.copy()
    mirror[:, 1] *= -1.0
    shape = (2 * facet_rows, 2 * BU)
    bands = np.concatenate([direct.reshape(shape), mirror.reshape(shape)], axis=1)
    a = angles(N1, N1 // 2, N1)
    c, s = np.cos(a), np.sin(a)
    lead = np.block([[c, s], [-s, c]])
    a = angles(N2, N2, N2)
    tail = np.stack([np.cos(a), np.sin(a)])
    a = angles(N1, N2, N1 * N2)
    twist = np.stack([np.cos(a), np.sin(a)]).astype(np.float32)
    return {
        "forward": np_split(bands * dirty_scale),
        "backward": np_split(bands.T * back_scale),
        "lead": np_split(lead),
        "lead_back": np_split(lead.T),
        "tail": np_split(tail),
        "twist": twist,
        "twist_back": twist.transpose(0, 2, 1).copy(),
    }


def bumps(cell, centre, half, scale, length):
    line = lax.broadcasted_iota(jnp.int32, (length, cell.shape[1]), 0).astype(F32)
    d = line - centre
    return jnp.where(jnp.abs(line - cell) <= half, jnp.exp(d * d * scale), 0.0)


def window(cell, fraction, half, scale):
    block = jnp.floor((cell - half) * (1.0 / BLOCK))
    near = cell - block * BLOCK
    wide = jnp.broadcast_to(block, (BLOCK, block.shape[1])).astype(BF16)
    return wide, bumps(near, near + fraction, half, scale, 2 * BLOCK)


def place_window(wide, fine, length):
    zero = jnp.zeros_like(fine[:BLOCK])
    out = []
    before = None
    for b in range(length // BLOCK):
        here = wide == b
        piece = zero if before is None else jnp.where(before, fine[BLOCK:], zero)
        out.append(jnp.where(here, fine[:BLOCK], piece))
        before = here
    return jnp.concatenate(out, axis=0)


def pack_body(vis, pos, row, col, cls, out):
    rows = row.shape[0]
    for part in range(2):
        out[pl.ds(part, rows, stride=8), :] = vis[part]
        out[pl.ds(2 + part, rows, stride=8), :] = pos[part]
    out[pl.ds(4, rows, stride=8), :] = row[...].astype(F32)
    out[pl.ds(5, rows, stride=8), :] = col[...].astype(F32)
    out[pl.ds(6, rows, stride=8), :] = cls[...].astype(F32)
    out[pl.ds(7, rows, stride=8), :] = jnp.zeros((rows, row.shape[1]), F32)


def pack(vis, pos, row, col, cls):
    return pl.pallas_call(
        pack_body,
        out_shape=jax.ShapeDtypeStruct((8 * row.shape[0], row.shape[1]), F32),
        name="pack",
    )(vis, pos, row, col, cls)


def build_table(got, tab):
    senders = got.shape[0] // 8
    slots = got.shape[1]
    half_n = senders // 2
    for side in range(2):
        spot = slice(side * slots, (side + 1) * slots)
        spot_low = slice((2 + side) * slots, (3 + side) * slots)

        def plane(k):
            return got[pl.ds(8 * side + k, half_n, stride=16), :]

        for k in range(4):
            high, low = split(plane(k))
            tab[k * half_n : (k + 1) * half_n, spot] = high
            tab[k * half_n : (k + 1) * half_n, spot_low] = low
        tab[4 * half_n :, spot] = ((plane(4) * 4.0 + plane(6)) * 256.0).astype(BF16)
        tab[4 * half_n :, spot_low] = plane(5).astype(BF16)


def gather_list(slot, tab):
    cap = slot.shape[1]
    half_n = tab.shape[0] // 5
    places = tab.shape[1] // 2
    line = lax.broadcasted_iota(jnp.int32, (half_n, cap), 0)
    low_line = lax.broadcasted_iota(jnp.int32, (places, cap), 0).astype(BF16)
    upper = lax.shift_right_logical(slot, 8)
    lower = lax.bitwise_and(slot, 255).astype(F32).astype(BF16)
    pick = jnp.where(low_line == lower, jnp.asarray(1.0, BF16), jnp.asarray(0.0, BF16))
    found = mm(tab[...], jnp.concatenate([pick, pick], axis=0), NN)
    mine = line == upper
    vals = [
        jnp.sum(jnp.where(mine, found[k * half_n : (k + 1) * half_n], 0.0), axis=0, keepdims=True) for k in range(5)
    ]
    code = vals[4].astype(jnp.int32)
    cell_col = lax.bitwise_and(code, 255).astype(F32)
    cell_row = lax.shift_right_logical(code, 10).astype(F32)
    half = lax.bitwise_and(lax.shift_right_logical(code, 8), 3).astype(F32) + 1.0
    return jnp.concatenate([cell_row, vals[2], cell_col, vals[3], half, vals[0], vals[1], slot.astype(F32)], axis=0)


def oriented(feat, flip):
    sign = 1.0 - 2.0 * flip.astype(F32)
    shift = flip.astype(F32) * N2
    half = feat[4:5]
    return feat[2:3] * sign + shift, feat[3:4] * sign, half, GAUSS / (half * half)


def grid_list(feat, flip):
    cell_col, offset, half, scale = oriented(feat, flip)
    wide, fine = window(feat[0:1], feat[1:2], half, scale)
    parts = [split(fine * feat[k : k + 1]) for k in (5, 6)]
    weighted = jnp.concatenate(
        [place_window(wide, parts[part][piece], BU) for piece in range(2) for part in range(2)], axis=0
    )
    wide, fine = window(cell_col, offset, half, scale)
    ch, cl = [place_window(wide, piece, N2 + BLOCK) for piece in split(fine)]
    both = mm(ch, weighted, NT)
    cross = mm(cl, weighted[: 2 * BU], NT)
    return both[:, : 2 * BU] + (both[:, 2 * BU :] + cross)


def gather_body(meta, lists, got, feats, tab):
    tiles = feats.shape[0]
    build_table(got, tab)
    for r in range(tiles):
        feats[r] = gather_list(lists[(1 - meta[0]) * tiles + r], tab)


def own_body(meta, lists, got, feats, acc, tab):
    tiles = feats.shape[0]
    high = meta[0]
    build_table(got, tab)
    for r in range(tiles):
        feat = gather_list(lists[high * tiles + own_tile(r, high)], tab)
        feats[r] = feat
        acc[r] = grid_list(feat, high)


def own_tile(r, high):
    return r + high * (3 - 2 * r)


def guest_tile(r, high):
    return own_tile(r, 1 - high)


def whole_call(body, args, out_shape, scratch, name):
    whole = pl.BlockSpec(memory_space=pltpu.VMEM)
    return pl.pallas_call(
        body,
        in_specs=[pl.BlockSpec(memory_space=pltpu.SMEM)] + [whole] * (len(args) - 1),
        out_specs=jax.tree.map(lambda _: whole, out_shape),
        out_shape=out_shape,
        scratch_shapes=scratch,
        compiler_params=pltpu.CompilerParams(vmem_limit_bytes=VMEM_BYTES),
        name=name,
    )(*[args[0]] + [pltpu.with_memory_space_constraint(x, pltpu.VMEM) for x in args[1:]])


def gather_lists(meta, lists, got, tiles):
    return whole_call(
        gather_body,
        (meta, lists, got),
        jax.ShapeDtypeStruct((tiles, 8, lists.shape[2]), F32),
        [pltpu.VMEM((5 * got.shape[0] // 16, 4 * got.shape[1]), BF16)],
        "gather_lists",
    )


def grid_own(meta, lists, got, tiles):
    return whole_call(
        own_body,
        (meta, lists, got),
        [
            jax.ShapeDtypeStruct((tiles, 8, lists.shape[2]), F32),
            jax.ShapeDtypeStruct((tiles, N2 + BLOCK, 2 * BU), F32),
        ],
        [pltpu.VMEM((5 * got.shape[0] // 16, 4 * got.shape[1]), BF16)],
        "grid_own",
    )


def guest_body(meta, feats, own, forward, out):
    high = meta[0]
    owners = out.shape[0]
    tiles = feats.shape[0]
    swap = high == 1
    carry = jnp.zeros((BLOCK, 4 * BU), F32)
    for r in range(tiles):
        guest = grid_list(feats[guest_tile(r, high)], 1 - high)
        mine = own[r]
        acc = jnp.concatenate([jnp.where(swap, guest, mine), jnp.where(swap, mine, guest)], axis=1)
        main = jnp.concatenate([acc[:BLOCK] + carry, acc[BLOCK:N2]], axis=0)
        carry = acc[N2:]
        bands = mm3(forward[...], main, NT)
        for h in range(2):
            out[:, 2 * r + h] = bands[:, h * LANES : (h + 1) * LANES].reshape(owners, 8, LANES)
    edge = mm3(forward[...], carry, NT)
    edge = jnp.concatenate([edge, jnp.zeros((edge.shape[0], LANES - BLOCK), F32)], axis=1)
    out[:, 2 * tiles] = edge.reshape(owners, 8, LANES)


def grid_guest(meta, feats, own, forward, owners):
    shape = (owners, 2 * feats.shape[0] + 1, 8, LANES)
    return whole_call(guest_body, (meta, feats, own, forward), jax.ShapeDtypeStruct(shape, F32), [], "grid_guest")


def transform_body(clip, got, model, lead, lead_back, tail, twist, twist_back, updated, out, xs, zs, *, rows):
    pairs = xs.shape[0] // 128
    owners = 2 * pairs
    half_n = N1 // 2
    span = pairs * 64
    plane = model.shape[0] // 2
    tc, ts = twist[0], twist[1]
    bc, bs = twist_back[0], twist_back[1]
    wide = jnp.concatenate([tail[0], tail[1]], axis=1)
    tall = jnp.concatenate([tail[k, p * N2 : (p + 1) * N2] for p in range(2) for k in range(2)], axis=0)
    lane = lax.broadcasted_iota(jnp.int32, (1, N1), 1)
    flip = jnp.where(lax.bitwise_and(lane, 1) == 0, 1.0, -1.0)
    row_id = lax.broadcasted_iota(jnp.int32, (8, LANES), 0)

    def place(q, g):
        return g if q == 0 else owners - 1 - g

    for q in range(2):
        for g in range(pairs):
            src = place(q, g) * 72
            dst = q * span + g * 64
            first = got[src : src + 8, :]
            if g > 0:
                past = place(q, g - 1) * 72 + 64
                first = first + got[past : past + 8, :]
            xs[dst : dst + 8, :] = first
            xs[dst + 8 : dst + 64, :] = got[src + 8 : src + 64, :]
    for q in range(2):
        level = clip[q]
        middle = place(q, pairs - 1) * 72 + 64
        edge = jnp.zeros((8, LANES), F32)
        for l in range(0, rows, 2):
            turned = []
            for k in range(2):
                parts = [
                    jnp.concatenate(
                        [xs[pl.ds(q * span + h * 8 + part * rows + l + k, half_n, stride=16), :] for h in range(2)],
                        axis=1,
                    )
                    for part in range(2)
                ]
                y = mm3(lead[...], jnp.concatenate(parts, axis=0), NN)
                yr, yi = y[:N1], y[N1:]
                turned.append(jnp.concatenate([yr * tc + yi * ts, yi * tc - yr * ts], axis=1))
            dirty = mm3(wide, jnp.concatenate(turned, axis=0), NT)
            news = []
            for k in range(2):
                part = dirty[:, k * N1 : (k + 1) * N1] + flip * got[middle + l + k : middle + l + k + 1, 0:1]
                prior = model[pl.ds(q * plane + l + k, N2, stride=rows), :]
                new = prior + LOOP_GAIN * (part - jnp.clip(part, -level, level))
                updated[pl.ds(q * plane + l + k, N2, stride=rows), :] = new
                news.append(new)
            a = mm3(tall, jnp.concatenate(news, axis=1), NN)
            for k in range(2):
                ar, ai = a[:N2, k * N1 : (k + 1) * N1], a[N2:, k * N1 : (k + 1) * N1]
                last = jnp.sum(ar[0:1] * flip, axis=1, keepdims=True)
                edge = jnp.where(row_id == l + k, last, edge)
                back = jnp.concatenate([ar * bc - ai * bs, ar * bs + ai * bc], axis=1)
                z = mm3(lead_back[...], back, NT)
                for part in range(2):
                    for h in range(2):
                        zs[pl.ds(q * span + h * 8 + part * rows + l + k, half_n, stride=16), :] = z[
                            part * half_n : (part + 1) * half_n, h * LANES : (h + 1) * LANES
                        ]
        for g in range(pairs):
            src = q * span + g * 64
            dst = place(q, g) * 72
            out[dst : dst + 64, :] = zs[src : src + 64, :]
            out[dst + 64 : dst + 72, :] = zs[src + 64 : src + 72, :] if g + 1 < pairs else edge


def transform(clip, got, model, consts, rows, owners):
    def body(*refs):
        transform_body(*refs, rows=rows)

    whole = pl.BlockSpec(memory_space=pltpu.VMEM)
    span = owners // 2 * 64
    return pl.pallas_call(
        body,
        in_specs=[pl.BlockSpec(memory_space=pltpu.SMEM)] + [whole] * 7,
        out_specs=[whole, whole],
        out_shape=[
            jax.ShapeDtypeStruct(model.shape, F32),
            jax.ShapeDtypeStruct(got.shape, F32),
        ],
        scratch_shapes=[pltpu.VMEM((2 * span, LANES), F32), pltpu.VMEM((2 * span, LANES), F32)],
        compiler_params=pltpu.CompilerParams(vmem_limit_bytes=VMEM_BYTES),
        name="transform",
    )(
        clip,
        *[
            pltpu.with_memory_space_constraint(x, pltpu.VMEM)
            for x in (got, model, *[consts[k] for k in ("lead", "lead_back", "tail", "twist", "twist_back")])
        ],
    )


def degrid_list(feat, pred, turn, spot, slots):
    one, none = jnp.asarray(1.0, BF16), jnp.asarray(0.0, BF16)
    slot = feat[7:8].astype(jnp.int32)
    sender = lax.shift_right_logical(slot, 7).astype(F32).astype(BF16)
    place = lax.bitwise_and(slot, slots - 1).astype(F32).astype(BF16)
    cell_col, offset, half, scale = oriented(feat, turn)
    rows = bumps(feat[0:1], feat[0:1] + feat[1:2], half, scale, BU)
    wide, fine = window(cell_col, offset, half, scale)
    ch, cl = [place_window(wide, piece, N2) for piece in split(fine)]
    ph, pw = split(pred[:, :N2])
    both = mm(jnp.concatenate([ph, pw], axis=0), ch, NN)
    t = both[: 2 * BU] + (both[2 * BU :] + mm(ph, cl, NN))
    gap = N2 - cell_col
    past = gap - offset
    rim = jnp.where(jnp.abs(gap) <= half, jnp.exp(past * past * scale), 0.0)
    t = t + pred[:, N2 : N2 + 1] * rim
    pick = jnp.where(spot == place, one, none)
    mine = spot == sender
    sides = []
    for part in range(2):
        val = jnp.sum(t[part * BU : (part + 1) * BU] * rows, axis=0, keepdims=True)
        for piece in split(val):
            sides.append(jnp.where(mine, piece, none))
    return mm(jnp.concatenate(sides, axis=0), pick, NT)


def degrid_body(meta, feats, guest_feats, got, backward, out):
    high = meta[0]
    slots = out.shape[1]
    senders = out.shape[0] // 4
    tiles, _, cap = feats.shape
    owners = got.shape[0]
    swap = high == 1
    spot = lax.broadcasted_iota(jnp.int32, (senders, cap), 0).astype(BF16)
    sums = [None, None]
    for r in range(tiles):
        columns = jnp.concatenate([got[:, 2 * r + h].reshape(owners * 8, LANES) for h in range(3)], axis=1)
        pred = mm3(backward[...], columns, NN)
        direct, mirror = pred[: 2 * BU], pred[2 * BU :]
        spread = (
            degrid_list(feats[r], jnp.where(swap, mirror, direct), high, spot, slots),
            degrid_list(guest_feats[guest_tile(r, high)], jnp.where(swap, direct, mirror), 1 - high, spot, slots),
        )
        sums = [new if old is None else old + new for old, new in zip(sums, spread)]
    for which in range(2):
        for part in range(2):
            lo = 2 * part * senders
            total = sums[which][lo : lo + senders] + sums[which][lo + senders : lo + 2 * senders]
            out[pl.ds(2 * which + part, senders, stride=4), :] = total


def degrid(meta, feats, guest_feats, got, backward, senders, slots):
    return whole_call(
        degrid_body,
        (meta, feats, guest_feats, got, backward),
        jax.ShapeDtypeStruct((4 * senders, slots), F32),
        [],
        "degrid_tiles",
    )


def finish_body(vis, got, counts, out, turned, *, group):
    rows, slots = got.shape[0] // 4, got.shape[1]
    owners = rows // group
    step = 4 * group
    for f in range(owners):
        lo = (owners - 1 - f) * step
        turned[f * step : (f + 1) * step, :] = got[lo : lo + step, :]
    limit = jnp.broadcast_to(counts[...], (rows, rows)).T[:, :slots]
    lane = lax.broadcasted_iota(jnp.int32, (rows, slots), 1)
    for part in range(2):
        back = got[pl.ds(part, rows, stride=4), :] + turned[pl.ds(2 + part, rows, stride=4), :]
        out[part] = jnp.where(lane < limit, vis[part] - back, 0.0)


def finish(vis, got, counts, group):
    def body(*refs):
        finish_body(*refs, group=group)

    return pl.pallas_call(
        body,
        out_shape=jax.ShapeDtypeStruct(vis.shape, F32),
        scratch_shapes=[pltpu.VMEM(got.shape, F32)],
        name="finish",
    )(vis, got, counts)


def per_device(
    visibilities,
    positions,
    cell_row,
    cell_column,
    kernel_class,
    send_counts,
    tile_lists,
    tile_counts,
    model_image,
    threshold,
):
    owners = lax.axis_size("fft")
    group = lax.axis_size("chan")
    senders = owners * group
    slots = visibilities.shape[3]
    channels, row_local, grid_side = model_image.shape
    cap = tile_lists.shape[2]
    tiles = tile_lists.shape[1] // channels
    facet_rows = row_local * owners
    dirty_scale = 1.0 / math.sqrt(owners * tiles * cap)
    back_scale = 0.5 / math.sqrt(facet_rows * grid_side)
    consts = {k: jnp.asarray(v) for k, v in tables(facet_rows, row_local, grid_side, dirty_scale, back_scale).items()}
    swap = [(i, owners - 1 - i) for i in range(owners)]
    meta = (lax.axis_index("fft") >= owners // 2).astype(jnp.int32).reshape(1)
    live = jnp.arange(cap, dtype=jnp.int32)[None, :] < tile_counts[0][:, None]
    lists = jnp.where(live, tile_lists[0], senders * slots)[:, None, :]

    payload = pack(visibilities[0], positions[0], cell_row[0], cell_column[0], kernel_class[0])
    got = lax.all_to_all(
        payload.reshape(senders, 8, slots), ("fft", "chan"), split_axis=0, concat_axis=0, tiled=True
    ).reshape(8 * senders, slots)

    def exchange(x):
        return lax.all_to_all(x, "fft", split_axis=0, concat_axis=0, tiled=True)

    guest_feats = lax.ppermute(gather_lists(meta, lists, got, tiles), "fft", swap)
    feats, own = grid_own(meta, lists, got, tiles)
    rows = exchange(grid_guest(meta, guest_feats, own, consts["forward"], owners))
    blocks = 2 * tiles + 1
    models = model_image.reshape(channels, row_local, N2, N1).transpose(0, 2, 1, 3)
    models = models.reshape(channels * N2 * row_local, N1)
    updated, back = transform(threshold, rows.reshape(owners * blocks * 8, LANES), models, consts, row_local, owners)
    cols = exchange(back.reshape(owners, blocks, 8, LANES))
    returned = degrid(meta, feats, guest_feats, cols, consts["backward"], senders, slots)
    back = lax.all_to_all(
        returned.reshape(senders, 4, slots), ("fft", "chan"), split_axis=0, concat_axis=0, tiled=True
    )
    residuals = finish(visibilities[0], back.reshape(4 * senders, slots), send_counts, group)
    updated = updated.reshape(channels, N2, row_local, N1).transpose(0, 2, 1, 3)
    return (updated.reshape(model_image.shape), residuals[None])


def solution(mesh):
    placed = (
        P(("fft", "chan"), None, None, None),
        P(("fft", "chan"), None, None, None),
        P(("fft", "chan"), None, None),
        P(("fft", "chan"), None, None),
        P(("fft", "chan"), None, None),
        P(("fft", "chan"), None),
        P(("fft", "chan"), None, None),
        P(("fft", "chan"), None),
        P("chan", "fft", None),
        P("chan"),
    )
    return jax.shard_map(
        per_device,
        mesh=mesh,
        in_specs=placed,
        out_specs=(P("chan", "fft", None), P(("fft", "chan"), None, None, None)),
        check_vma=False,
    )
```

```python
import math

import jax
import jax.numpy as jnp
import numpy as np
from jax import lax
from jax.experimental import pallas as pl
from jax.experimental.pallas import tpu as pltpu
from jax.sharding import PartitionSpec as P

BU = 64
LOOP_GAIN = 0.7
N1 = 128
N2 = 256
LANES = 128
BLOCK = 16
F32 = jnp.float32
BF16 = jnp.bfloat16
GAUSS = -1.0 / 0.72
VMEM_BYTES = 36 * 1024 * 1024

NN = (((1,), (0,)), ((), ()))
NT = (((1,), (1,)), ((), ()))


def split(x):
    high = x.astype(BF16)
    low = (x - high.astype(F32)).astype(BF16)
    return high, low


def mm(a, b, dims):
    return lax.dot_general(a, b, dims, preferred_element_type=F32)


def mm3(table, b, dims):
    m = table.shape[0] // 2
    high, low = split(b)
    both = mm(table, high, dims)
    return both[:m] + (both[m:] + mm(table[:m], low, dims))


def np_split(x):
    x = np.asarray(x, np.float32)
    high = x.astype(jnp.bfloat16)
    low = (x - high.astype(np.float32)).astype(jnp.bfloat16)
    return np.concatenate([high, low], axis=-2)


def angles(rows, cols, modulus):
    product = np.arange(rows, dtype=np.int64)[:, None] * np.arange(cols, dtype=np.int64)[None, :] % modulus
    return 2.0 * np.pi / modulus * product


def tables(facet_rows, row_local, grid_side, dirty_scale, back_scale):
    phase = (grid_side // 2 + np.arange(BU))[None, :] * np.arange(facet_rows)[:, None] % facet_rows
    theta = 2.0 * np.pi / facet_rows * phase
    c, s = np.cos(theta), np.sin(theta)
    owners = facet_rows // row_local
    direct = np.zeros((owners, 2, row_local, 2, BU))
    cc, ss = c.reshape(owners, row_local, BU), s.reshape(owners, row_local, BU)
    direct[:, 0, :, 0], direct[:, 0, :, 1] = cc, ss
    direct[:, 1, :, 0], direct[:, 1, :, 1] = -ss, cc
    mirror = direct.copy()
    mirror[:, 1] *= -1.0
    shape = (2 * facet_rows, 2 * BU)
    bands = np.concatenate([direct.reshape(shape), mirror.reshape(shape)], axis=1)
    a = angles(N1, N1 // 2, N1)
    c, s = np.cos(a), np.sin(a)
    lead = np.block([[c, s], [-s, c]])
    a = angles(N2, N2, N2)
    tail = np.stack([np.cos(a), np.sin(a)])
    a = angles(N1, N2, N1 * N2)
    twist = np.stack([np.cos(a), np.sin(a)]).astype(np.float32)
    return {
        "forward": np_split(bands * dirty_scale),
        "backward": np_split(bands.T * back_scale),
        "lead": np_split(lead),
        "lead_back": np_split(lead.T),
        "tail": np_split(tail),
        "twist": twist,
        "twist_back": twist.transpose(0, 2, 1).copy(),
    }


def bumps(cell, centre, half, scale, length):
    line = lax.broadcasted_iota(jnp.int32, (length, cell.shape[1]), 0).astype(F32)
    d = line - centre
    return jnp.where(jnp.abs(line - cell) <= half, jnp.exp(d * d * scale), 0.0)


def window(cell, fraction, half, scale):
    block = jnp.floor((cell - half) * (1.0 / BLOCK))
    near = cell - block * BLOCK
    wide = jnp.broadcast_to(block, (BLOCK, block.shape[1])).astype(BF16)
    return wide, bumps(near, near + fraction, half, scale, 2 * BLOCK)


def place_window(wide, fine, length):
    zero = jnp.zeros_like(fine[:BLOCK])
    out = []
    before = None
    for b in range(length // BLOCK):
        here = wide == b
        piece = zero if before is None else jnp.where(before, fine[BLOCK:], zero)
        out.append(jnp.where(here, fine[:BLOCK], piece))
        before = here
    return jnp.concatenate(out, axis=0)


def pack_body(vis, pos, row, col, cls, out):
    rows = row.shape[0]
    for part in range(2):
        out[pl.ds(part, rows, stride=8), :] = vis[part]
        out[pl.ds(2 + part, rows, stride=8), :] = pos[part]
    out[pl.ds(4, rows, stride=8), :] = row[...].astype(F32)
    out[pl.ds(5, rows, stride=8), :] = col[...].astype(F32)
    out[pl.ds(6, rows, stride=8), :] = cls[...].astype(F32)
    out[pl.ds(7, rows, stride=8), :] = jnp.zeros((rows, row.shape[1]), F32)


def pack(vis, pos, row, col, cls):
    return pl.pallas_call(
        pack_body,
        out_shape=pltpu.VMEM((8 * row.shape[0], row.shape[1]), F32),
        name="pack",
    )(vis, pos, row, col, cls)


def build_table(got, tab):
    senders = got.shape[0] // 8
    slots = got.shape[1]
    half_n = senders // 2
    for side in range(2):
        spot = slice(side * slots, (side + 1) * slots)
        spot_low = slice((2 + side) * slots, (3 + side) * slots)

        def plane(k):
            return got[pl.ds(8 * side + k, half_n, stride=16), :]

        for k in range(4):
            high, low = split(plane(k))
            tab[k * half_n : (k + 1) * half_n, spot] = high
            tab[k * half_n : (k + 1) * half_n, spot_low] = low
        tab[4 * half_n :, spot] = ((plane(4) * 4.0 + plane(6)) * 256.0).astype(BF16)
        tab[4 * half_n :, spot_low] = plane(5).astype(BF16)


def gather_list(slot, tab):
    cap = slot.shape[1]
    half_n = tab.shape[0] // 5
    places = tab.shape[1] // 2
    line = lax.broadcasted_iota(jnp.int32, (half_n, cap), 0)
    low_line = lax.broadcasted_iota(jnp.int32, (places, cap), 0).astype(BF16)
    upper = lax.shift_right_logical(slot, 8)
    lower = lax.bitwise_and(slot, 255).astype(F32).astype(BF16)
    pick = jnp.where(low_line == lower, jnp.asarray(1.0, BF16), jnp.asarray(0.0, BF16))
    found = mm(tab[...], jnp.concatenate([pick, pick], axis=0), NN)
    mine = line == upper
    vals = [
        jnp.sum(jnp.where(mine, found[k * half_n : (k + 1) * half_n], 0.0), axis=0, keepdims=True) for k in range(5)
    ]
    code = vals[4].astype(jnp.int32)
    cell_col = lax.bitwise_and(code, 255).astype(F32)
    cell_row = lax.shift_right_logical(code, 10).astype(F32)
    half = lax.bitwise_and(lax.shift_right_logical(code, 8), 3).astype(F32) + 1.0
    return jnp.concatenate([cell_row, vals[2], cell_col, vals[3], half, vals[0], vals[1], slot.astype(F32)], axis=0)


def oriented(feat, flip):
    sign = 1.0 - 2.0 * flip.astype(F32)
    shift = flip.astype(F32) * N2
    half = feat[4:5]
    return feat[2:3] * sign + shift, feat[3:4] * sign, half, GAUSS / (half * half)


def grid_list(feat, flip):
    cell_col, offset, half, scale = oriented(feat, flip)
    wide, fine = window(feat[0:1], feat[1:2], half, scale)
    parts = [split(fine * feat[k : k + 1]) for k in (5, 6)]
    weighted = jnp.concatenate(
        [place_window(wide, parts[part][piece], BU) for piece in range(2) for part in range(2)], axis=0
    )
    wide, fine = window(cell_col, offset, half, scale)
    ch, cl = [place_window(wide, piece, N2 + BLOCK) for piece in split(fine)]
    both = mm(ch, weighted, NT)
    cross = mm(cl, weighted[: 2 * BU], NT)
    return both[:, : 2 * BU] + (both[:, 2 * BU :] + cross)


def gather_body(meta, lists, got, feats, tab):
    tiles = feats.shape[0]
    build_table(got, tab)
    cap = feats.shape[2]
    slots = jnp.concatenate([lists[(1 - meta[0]) * tiles + r] for r in range(tiles)], axis=1)
    found = gather_list(slots, tab)
    for r in range(tiles):
        feats[r] = found[:, r * cap : (r + 1) * cap]


def own_body(meta, lists, got, feats, acc, tab):
    tiles = feats.shape[0]
    high = meta[0]
    build_table(got, tab)
    cap = feats.shape[2]
    slots = jnp.concatenate([lists[high * tiles + own_tile(r, high)] for r in range(tiles)], axis=1)
    found = gather_list(slots, tab)
    for r in range(tiles):
        feat = found[:, r * cap : (r + 1) * cap]
        feats[r] = feat
        acc[r] = grid_list(feat, high)


def own_tile(r, high):
    return r + high * (3 - 2 * r)


def guest_tile(r, high):
    return own_tile(r, 1 - high)


def whole_call(body, args, out_shape, scratch, name):
    whole = pl.BlockSpec(memory_space=pltpu.VMEM)
    return pl.pallas_call(
        body,
        in_specs=[pl.BlockSpec(memory_space=pltpu.SMEM)] + [whole] * (len(args) - 1),
        out_specs=jax.tree.map(lambda _: whole, out_shape),
        out_shape=jax.tree.map(lambda o: pltpu.VMEM(o.shape, o.dtype), out_shape),
        scratch_shapes=scratch,
        compiler_params=pltpu.CompilerParams(vmem_limit_bytes=VMEM_BYTES),
        name=name,
    )(*[args[0]] + [pltpu.with_memory_space_constraint(x, pltpu.VMEM) for x in args[1:]])


def gather_lists(meta, lists, got, tiles):
    return whole_call(
        gather_body,
        (meta, lists, got),
        jax.ShapeDtypeStruct((tiles, 8, lists.shape[2]), F32),
        [pltpu.VMEM((5 * got.shape[0] // 16, 4 * got.shape[1]), BF16)],
        "gather_lists",
    )


def grid_own(meta, lists, got, tiles):
    return whole_call(
        own_body,
        (meta, lists, got),
        [
            jax.ShapeDtypeStruct((tiles, 8, lists.shape[2]), F32),
            jax.ShapeDtypeStruct((tiles, N2 + BLOCK, 2 * BU), F32),
        ],
        [pltpu.VMEM((5 * got.shape[0] // 16, 4 * got.shape[1]), BF16)],
        "grid_own",
    )


def guest_body(meta, feats, own, forward, out):
    high = meta[0]
    owners = out.shape[0]
    tiles = feats.shape[0]
    swap = high == 1
    carry = jnp.zeros((BLOCK, 4 * BU), F32)
    for r in range(tiles):
        guest = grid_list(feats[guest_tile(r, high)], 1 - high)
        mine = own[r]
        acc = jnp.concatenate([jnp.where(swap, guest, mine), jnp.where(swap, mine, guest)], axis=1)
        main = jnp.concatenate([acc[:BLOCK] + carry, acc[BLOCK:N2]], axis=0)
        carry = acc[N2:]
        bands = mm3(forward[...], main, NT)
        for h in range(2):
            out[:, 2 * r + h] = bands[:, h * LANES : (h + 1) * LANES].reshape(owners, 8, LANES)
    edge = mm3(forward[...], carry, NT)
    edge = jnp.concatenate([edge, jnp.zeros((edge.shape[0], LANES - BLOCK), F32)], axis=1)
    out[:, 2 * tiles] = edge.reshape(owners, 8, LANES)


def grid_guest(meta, feats, own, forward, owners):
    shape = (owners, 2 * feats.shape[0] + 1, 8, LANES)
    return whole_call(guest_body, (meta, feats, own, forward), jax.ShapeDtypeStruct(shape, F32), [], "grid_guest")


def transform_body(clip, got, model, lead, lead_back, tail, twist, twist_back, updated, out, xs, zs, *, rows):
    pairs = xs.shape[0] // 128
    owners = 2 * pairs
    half_n = N1 // 2
    span = pairs * 64
    plane = model.shape[0] // 2
    tc, ts = twist[0], twist[1]
    bc, bs = twist_back[0], twist_back[1]
    wide = jnp.concatenate([tail[0], tail[1]], axis=1)
    tall = jnp.concatenate([tail[k, p * N2 : (p + 1) * N2] for p in range(2) for k in range(2)], axis=0)
    lane = lax.broadcasted_iota(jnp.int32, (1, N1), 1)
    flip = jnp.where(lax.bitwise_and(lane, 1) == 0, 1.0, -1.0)
    row_id = lax.broadcasted_iota(jnp.int32, (8, LANES), 0)

    def place(q, g):
        return g if q == 0 else owners - 1 - g

    for q in range(2):
        for g in range(pairs):
            src = place(q, g) * 72
            dst = q * span + g * 64
            first = got[src : src + 8, :]
            if g > 0:
                past = place(q, g - 1) * 72 + 64
                first = first + got[past : past + 8, :]
            xs[dst : dst + 8, :] = first
            xs[dst + 8 : dst + 64, :] = got[src + 8 : src + 64, :]
    items = [(q, l) for q in range(2) for l in range(rows)]
    loaded = []
    for q, l in items:
        parts = [
            jnp.concatenate(
                [xs[pl.ds(q * span + h * 8 + part * rows + l, half_n, stride=16), :] for h in range(2)], axis=1
            )
            for part in range(2)
        ]
        loaded.append(jnp.concatenate(parts, axis=0))
    y = mm3(lead[...], jnp.concatenate(loaded, axis=1), NN)
    turned = []
    for k in range(len(items)):
        yr, yi = y[:N1, k * N2 : (k + 1) * N2], y[N1:, k * N2 : (k + 1) * N2]
        turned.append(jnp.concatenate([yr * tc + yi * ts, yi * tc - yr * ts], axis=1))
    dirty = mm3(wide, jnp.concatenate(turned, axis=0), NT)
    news = []
    for k, (q, l) in enumerate(items):
        level = clip[q]
        middle = place(q, pairs - 1) * 72 + 64 + l
        part = dirty[:, k * N1 : (k + 1) * N1] + flip * got[middle : middle + 1, 0:1]
        prior = model[pl.ds(q * plane + l, N2, stride=rows), :]
        new = prior + LOOP_GAIN * (part - jnp.clip(part, -level, level))
        updated[pl.ds(q * plane + l, N2, stride=rows), :] = new
        news.append(new)
    a = mm3(tall, jnp.concatenate(news, axis=1), NN)
    edges = [jnp.zeros((8, LANES), F32) for q in range(2)]
    back = []
    for k, (q, l) in enumerate(items):
        ar, ai = a[:N2, k * N1 : (k + 1) * N1], a[N2:, k * N1 : (k + 1) * N1]
        last = jnp.sum(ar[0:1] * flip, axis=1, keepdims=True)
        edges[q] = jnp.where(row_id == l, last, edges[q])
        back.append(jnp.concatenate([ar * bc - ai * bs, ar * bs + ai * bc], axis=1))
    z = mm3(lead_back[...], jnp.concatenate(back, axis=0), NT)
    for k, (q, l) in enumerate(items):
        for part in range(2):
            for h in range(2):
                zs[pl.ds(q * span + h * 8 + part * rows + l, half_n, stride=16), :] = z[
                    part * half_n : (part + 1) * half_n, k * N2 + h * LANES : k * N2 + (h + 1) * LANES
                ]
    for q in range(2):
        for g in range(pairs):
            src = q * span + g * 64
            dst = place(q, g) * 72
            out[dst : dst + 64, :] = zs[src : src + 64, :]
            out[dst + 64 : dst + 72, :] = zs[src + 64 : src + 72, :] if g + 1 < pairs else edges[q]


def transform(clip, got, model, consts, rows, owners):
    def body(*refs):
        transform_body(*refs, rows=rows)

    whole = pl.BlockSpec(memory_space=pltpu.VMEM)
    span = owners // 2 * 64
    return pl.pallas_call(
        body,
        in_specs=[pl.BlockSpec(memory_space=pltpu.SMEM)] + [whole] * 7,
        out_specs=[whole, whole],
        out_shape=[
            pltpu.VMEM(model.shape, F32),
            pltpu.VMEM(got.shape, F32),
        ],
        scratch_shapes=[pltpu.VMEM((2 * span, LANES), F32), pltpu.VMEM((2 * span, LANES), F32)],
        compiler_params=pltpu.CompilerParams(vmem_limit_bytes=VMEM_BYTES),
        name="transform",
    )(
        clip,
        *[
            pltpu.with_memory_space_constraint(x, pltpu.VMEM)
            for x in (got, model, *[consts[k] for k in ("lead", "lead_back", "tail", "twist", "twist_back")])
        ],
    )


def degrid_list(feat, pred, turn, spot):
    one, none = jnp.asarray(1.0, BF16), jnp.asarray(0.0, BF16)
    slot = feat[7:8].astype(jnp.int32)
    upper = lax.shift_right_logical(slot, 8).astype(F32).astype(BF16)
    lower = lax.bitwise_and(slot, 255).astype(F32).astype(BF16)
    cell_col, offset, half, scale = oriented(feat, turn)
    rows = bumps(feat[0:1], feat[0:1] + feat[1:2], half, scale, BU)
    wide, fine = window(cell_col, offset, half, scale)
    ch, cl = [place_window(wide, piece, N2) for piece in split(fine)]
    ph, pw = split(pred[:, :N2])
    both = mm(jnp.concatenate([ph, pw], axis=0), ch, NN)
    t = both[: 2 * BU] + (both[2 * BU :] + mm(ph, cl, NN))
    gap = N2 - cell_col
    past = gap - offset
    rim = jnp.where(jnp.abs(gap) <= half, jnp.exp(past * past * scale), 0.0)
    t = t + pred[:, N2 : N2 + 1] * rim
    pick = jnp.where(spot == lower, one, none)
    mine = spot[: spot.shape[0] // 4] == upper
    sides = []
    for part in range(2):
        val = jnp.sum(t[part * BU : (part + 1) * BU] * rows, axis=0, keepdims=True)
        for piece in split(val):
            sides.append(jnp.where(mine, piece, none))
    return mm(jnp.concatenate(sides, axis=0), pick, NT)


def degrid_body(meta, feats, guest_feats, got, backward, out):
    high = meta[0]
    slots = out.shape[1]
    senders = out.shape[0] // 4
    tiles, _, cap = feats.shape
    owners = got.shape[0]
    swap = high == 1
    spot = lax.broadcasted_iota(jnp.int32, (2 * slots, cap), 0).astype(BF16)
    sums = [None, None]
    for r in range(tiles):
        columns = jnp.concatenate([got[:, 2 * r + h].reshape(owners * 8, LANES) for h in range(3)], axis=1)
        pred = mm3(backward[...], columns, NN)
        direct, mirror = pred[: 2 * BU], pred[2 * BU :]
        spread = (
            degrid_list(feats[r], jnp.where(swap, mirror, direct), high, spot),
            degrid_list(guest_feats[guest_tile(r, high)], jnp.where(swap, direct, mirror), 1 - high, spot),
        )
        sums = [new if old is None else old + new for old, new in zip(sums, spread)]
    for which in range(2):
        for part in range(2):
            half_n = senders // 2
            lo = 2 * part * half_n
            total = sums[which][lo : lo + half_n] + sums[which][lo + half_n : lo + 2 * half_n]
            for side in range(2):
                spots = pl.ds(2 * which + part + 4 * side, half_n, stride=8)
                out[spots, :] = total[:, side * slots : (side + 1) * slots]


def degrid(meta, feats, guest_feats, got, backward, senders, slots):
    return whole_call(
        degrid_body,
        (meta, feats, guest_feats, got, backward),
        jax.ShapeDtypeStruct((4 * senders, slots), F32),
        [],
        "degrid_tiles",
    )


def finish_body(vis, got, counts, out, turned, *, group):
    rows, slots = got.shape[0] // 4, got.shape[1]
    owners = rows // group
    step = 4 * group
    for f in range(owners):
        lo = (owners - 1 - f) * step
        turned[f * step : (f + 1) * step, :] = got[lo : lo + step, :]
    limit = jnp.broadcast_to(counts[...], (rows, rows)).T[:, :slots]
    lane = lax.broadcasted_iota(jnp.int32, (rows, slots), 1)
    for part in range(2):
        back = got[pl.ds(part, rows, stride=4), :] + turned[pl.ds(2 + part, rows, stride=4), :]
        out[part] = jnp.where(lane < limit, vis[part] - back, 0.0)


def finish(vis, got, counts, group):
    def body(*refs):
        finish_body(*refs, group=group)

    return pl.pallas_call(
        body,
        out_shape=jax.ShapeDtypeStruct(vis.shape, F32),
        scratch_shapes=[pltpu.VMEM(got.shape, F32)],
        name="finish",
    )(*[pltpu.with_memory_space_constraint(x, pltpu.VMEM) for x in (vis, got, counts)])


def per_device(
    visibilities,
    positions,
    cell_row,
    cell_column,
    kernel_class,
    send_counts,
    tile_lists,
    tile_counts,
    model_image,
    threshold,
):
    owners = lax.axis_size("fft")
    group = lax.axis_size("chan")
    senders = owners * group
    slots = visibilities.shape[3]
    channels, row_local, grid_side = model_image.shape
    cap = tile_lists.shape[2]
    tiles = tile_lists.shape[1] // channels
    facet_rows = row_local * owners
    dirty_scale = 1.0 / math.sqrt(owners * tiles * cap)
    back_scale = 0.5 / math.sqrt(facet_rows * grid_side)
    consts = {k: jnp.asarray(v) for k, v in tables(facet_rows, row_local, grid_side, dirty_scale, back_scale).items()}
    swap = [(i, owners - 1 - i) for i in range(owners)]
    meta = (lax.axis_index("fft") >= owners // 2).astype(jnp.int32).reshape(1)
    live = jnp.arange(cap, dtype=jnp.int32)[None, :] < tile_counts[0][:, None]
    lists = jnp.where(live, tile_lists[0], senders * slots)[:, None, :]

    payload = pack(visibilities[0], positions[0], cell_row[0], cell_column[0], kernel_class[0])
    got = lax.all_to_all(
        payload.reshape(senders, 8, slots), ("fft", "chan"), split_axis=0, concat_axis=0, tiled=True
    ).reshape(8 * senders, slots)

    def exchange(x):
        return lax.all_to_all(x, "fft", split_axis=0, concat_axis=0, tiled=True)

    guest_feats = lax.ppermute(gather_lists(meta, lists, got, tiles), "fft", swap)
    feats, own = grid_own(meta, lists, got, tiles)
    rows = exchange(grid_guest(meta, guest_feats, own, consts["forward"], owners))
    blocks = 2 * tiles + 1
    models = model_image.reshape(channels, row_local, N2, N1).transpose(0, 2, 1, 3)
    models = models.reshape(channels * N2 * row_local, N1)
    updated, back = transform(threshold, rows.reshape(owners * blocks * 8, LANES), models, consts, row_local, owners)
    cols = exchange(back.reshape(owners, blocks, 8, LANES))
    returned = degrid(meta, feats, guest_feats, cols, consts["backward"], senders, slots)
    back = lax.all_to_all(
        returned.reshape(senders, 4, slots), ("fft", "chan"), split_axis=0, concat_axis=0, tiled=True
    )
    residuals = finish(visibilities[0], back.reshape(4 * senders, slots), send_counts, group)
    updated = updated.reshape(channels, N2, row_local, N1).transpose(0, 2, 1, 3)
    return (updated.reshape(model_image.shape), residuals[None])


def solution(mesh):
    placed = (
        P(("fft", "chan"), None, None, None),
        P(("fft", "chan"), None, None, None),
        P(("fft", "chan"), None, None),
        P(("fft", "chan"), None, None),
        P(("fft", "chan"), None, None),
        P(("fft", "chan"), None),
        P(("fft", "chan"), None, None),
        P(("fft", "chan"), None),
        P("chan", "fft", None),
        P("chan"),
    )
    return jax.shard_map(
        per_device,
        mesh=mesh,
        in_specs=placed,
        out_specs=(P("chan", "fft", None), P(("fft", "chan"), None, None, None)),
        check_vma=False,
    )
```
